128 devices in a mesh: uly: 4 (over x), blk: 32 (over z, y, core).
Axes of the slice: x: 4, y: 4, z: 4, core: 2. Of those that a mesh axis runs over, the one named last changes fastest.
Arguments:
- video_q: bfloat16 [36864, 3072], P(('blk', 'uly')), may hold values from -16 to 16
- video_k: bfloat16 [36864, 3072], P(('blk', 'uly')), may hold values from -16 to 16
- video_v: bfloat16 [36864, 3072], P(('blk', 'uly')), may hold values from -6 to 6
- text_q: bfloat16 [256, 3072], P('uly'), may hold values from -16 to 16
- text_k: bfloat16 [256, 3072], P('uly'), may hold values from -16 to 16
- text_v: bfloat16 [256, 3072], P('uly'), may hold values from -6 to 6
- window_tiles: int32 [96, 6], P('blk'), may hold values from 0 to 95, as said below
- text_len: int32 [1], replicated, may hold values from 64 to 256
Outputs:
- video_out: bfloat16 [36864, 3072], P(('blk', 'uly'))
- text_out: bfloat16 [256, 3072], P('uly')
The draws below stay inside these ranges and needn't reach their ends.
Inputs may be any that keep to these rules, and one draw needn't show every extreme that they name: `window_tiles`: tile j lies in time slice j // 3 of 32; row j lists, each once and in any order, the 6 tiles of two consecutive time slices, one of which is the slice of tile j.
All inputs are finite; a program needn't handle non-finite values.
Results may differ from the reference program's by a relative error of at most 0.0036.
Values may be sent and summed in bfloat16 or wider, within the bound.
No kernel may reach another device: no remote copies, remote signals or barrier semaphores. Data moves between devices by JAX's collectives and lax.ppermute only.
A program may use at most 128 MiB of HBM per device.

```python
import math
import jax
import jax.numpy as jnp
from jax import lax

HEADS = 24
D_HEAD = 128
TXT = 256
TILE = 384
TW_DEV = 3
WIN = 6
QTILES = 96
TSLICES = 32
VID = 36864


def lifted(key, row_count, col_count, label):
    spread = 1.6
    base = jax.random.fold_in(key, label)
    noise = jax.random.normal(jax.random.fold_in(base, 14), (row_count, col_count), jnp.float32)
    return spread * jnp.clip(noise, -6.0, 6.0)


def draw_video_q(key, part):
    return lifted(key, VID, HEADS * D_HEAD, 101).astype(jnp.bfloat16)


def draw_video_k(key, part):
    return lifted(key, VID, HEADS * D_HEAD, 202).astype(jnp.bfloat16)


def draw_text_q(key, part):
    return lifted(key, TXT, HEADS * D_HEAD, 303).astype(jnp.bfloat16)


def draw_text_k(key, part):
    return lifted(key, TXT, HEADS * D_HEAD, 404).astype(jnp.bfloat16)


def draw_window_tiles(key, part):
    positions = jnp.arange(QTILES, dtype=jnp.int32)
    time_slice = positions // TW_DEV
    coin_flip = jax.random.randint(jax.random.fold_in(key, 21), (QTILES,), 0, 2)
    first_slice = jnp.clip(time_slice - coin_flip, 0, TSLICES - 2)
    member = first_slice[:, None] * TW_DEV + jnp.arange(WIN, dtype=jnp.int32)[None, :]
    scores = jax.random.randint(jax.random.fold_in(key, 22), (QTILES, WIN), 0, 1 << 20) * WIN
    scores = scores + jnp.arange(WIN, dtype=jnp.int32)[None, :]
    ordering = jnp.argsort(scores, axis=1)
    return jnp.take_along_axis(member, ordering, axis=1).astype(jnp.int32)


def block_scale(stream_key, dims, shards, low, top_value):
    def one(position, shards_of):
        heights = jax.random.uniform(jax.random.fold_in(jax.random.fold_in(stream_key, 6), position), (shards_of,), jnp.float32, low / len(shards), top_value / len(shards))
        return jnp.repeat(jnp.exp(heights), dims[position] // shards_of).reshape((-1,) + (1,) * (len(dims) - position - 1))

    gain = one(*shards[0])
    for cut in shards[1:]:
        gain = gain * one(*cut)
    return gain


def gaussian(rng, shape, width, bound, split=(), kind=jnp.bfloat16):
    array = jax.random.normal(rng, shape, jnp.float32) * width
    if len(split) > 0:
        array = block_scale(rng, shape, split, -0.22, 0.18) * array
    return jnp.clip(array, min=-bound, max=bound).astype(kind)


def setup_inputs(seed: int = 0) -> dict:
    seeds = jax.random.split(jax.random.key(seed), 9)
    return {
        "video_q": draw_video_q(jax.random.fold_in(seeds[8], 71), 0),
        "video_k": draw_video_k(jax.random.fold_in(seeds[8], 71), 0),
        "video_v": gaussian(seeds[2], (VID, HEADS * D_HEAD), 1.0, 6.0, ((0, 128),)),
        "text_q": draw_text_q(jax.random.fold_in(seeds[8], 71), 0),
        "text_k": draw_text_k(jax.random.fold_in(seeds[8], 71), 0),
        "text_v": gaussian(seeds[5], (TXT, HEADS * D_HEAD), 1.0, 6.0, ((0, 4),)),
        "window_tiles": draw_window_tiles(jax.random.fold_in(seeds[8], 71), 0),
        "text_len": jax.random.randint(seeds[7], (1,), TXT // 4, TXT + 1).astype(jnp.int32),
    }


def round_bf(values):
    rounded = lax.optimization_barrier(values.astype(jnp.bfloat16))
    return rounded.astype(jnp.float32)

def reference(video_q, video_k, video_v, text_q, text_k, text_v, window_tiles, text_len):
    inv_root = 1.0 / math.sqrt(D_HEAD)
    tile_q = video_q.reshape(QTILES, TILE, HEADS, D_HEAD)
    tile_k = video_k.reshape(QTILES, TILE, HEADS, D_HEAD)
    tile_v = video_v.reshape(QTILES, TILE, HEADS, D_HEAD)
    text_keys = text_k.reshape(TXT, HEADS, D_HEAD).astype(jnp.float32)
    text_values = text_v.reshape(TXT, HEADS, D_HEAD).astype(jnp.float32)
    live_text = jnp.arange(TXT, dtype=jnp.int32) < text_len[0]

    def tile_attention(inputs):
        queries, chosen = inputs
        keys_win = jnp.take(tile_k, chosen, axis=0).reshape(WIN * TILE, HEADS, D_HEAD).astype(jnp.float32)
        values_win = jnp.take(tile_v, chosen, axis=0).reshape(WIN * TILE, HEADS, D_HEAD).astype(jnp.float32)
        queries_wide = queries.astype(jnp.float32)
        win_scores = jnp.einsum('qhd,khd->hqk', queries_wide, keys_win) * inv_root
        txt_scores = jnp.einsum('qhd,khd->hqk', queries_wide, text_keys) * inv_root
        txt_scores = jnp.where(live_text[None, None, :], txt_scores, -jnp.inf)
        row_top = jnp.maximum(lax.optimization_barrier(jnp.max(win_scores, axis=2)), lax.optimization_barrier(jnp.max(txt_scores, axis=2)))[:, :, None]
        win_weights = jnp.exp(win_scores - row_top)
        txt_weights = jnp.exp(txt_scores - row_top)
        weight_sum = lax.optimization_barrier(jnp.sum(win_weights, axis=2)) + lax.optimization_barrier(jnp.sum(txt_weights, axis=2))
        numerator = jnp.einsum('hqk,khd->hqd', round_bf(win_weights), values_win)
        numerator = numerator + jnp.einsum('hqk,khd->hqd', round_bf(txt_weights), text_values)
        result = numerator / weight_sum[:, :, None]
        return jnp.transpose(result, (1, 0, 2)).astype(jnp.bfloat16)
    video_out = lax.map(tile_attention, (tile_q, window_tiles)).reshape(VID, HEADS * D_HEAD)

    def text_attention(inputs):
        queries, keys_vid, values_vid, keys_txt, values_txt = inputs
        vid_scores = jnp.dot(queries, keys_vid.T, preferred_element_type=jnp.float32) * inv_root
        txt_scores = jnp.dot(queries, keys_txt.T, preferred_element_type=jnp.float32) * inv_root
        txt_scores = jnp.where(live_text[None, :], txt_scores, -jnp.inf)
        row_top = jnp.maximum(lax.optimization_barrier(jnp.max(vid_scores, axis=1)), lax.optimization_barrier(jnp.max(txt_scores, axis=1)))[:, None]
        vid_weights = jnp.exp(vid_scores - row_top)
        txt_weights = jnp.exp(txt_scores - row_top)
        weight_sum = lax.optimization_barrier(jnp.sum(vid_weights, axis=1)) + lax.optimization_barrier(jnp.sum(txt_weights, axis=1))
        numerator = jnp.dot(vid_weights.astype(jnp.bfloat16), values_vid, preferred_element_type=jnp.float32)
        numerator = numerator + jnp.dot(txt_weights.astype(jnp.bfloat16), values_txt, preferred_element_type=jnp.float32)
        return (numerator / weight_sum[:, None]).astype(jnp.bfloat16)
    per_head = (jnp.transpose(text_q.reshape(TXT, HEADS, D_HEAD), (1, 0, 2)), jnp.transpose(video_k.reshape(VID, HEADS, D_HEAD), (1, 0, 2)), jnp.transpose(video_v.reshape(VID, HEADS, D_HEAD), (1, 0, 2)), jnp.transpose(text_k.reshape(TXT, HEADS, D_HEAD), (1, 0, 2)), jnp.transpose(text_v.reshape(TXT, HEADS, D_HEAD), (1, 0, 2)))
    text_heads = lax.map(text_attention, per_head)
    text_out = jnp.transpose(text_heads, (1, 0, 2)).reshape(TXT, HEADS * D_HEAD)
    return (video_out, text_out)
```

```python
import functools
import math

import jax
import jax.numpy as jnp
from jax import lax
from jax.experimental import pallas as pl
from jax.experimental.pallas import tpu as pltpu
from jax.sharding import PartitionSpec as P

HEADS = 24
D = 128
TXT = 256
GROUP = 4
HD = HEADS // GROUP
ROWS = 288
SLICE = ROWS * GROUP
TILE = 384
TROWS = TXT // GROUP
BLK = 32
DEVS = GROUP * BLK
RB = 128
KEYS = 2 * SLICE + TXT
SCALE = math.log2(math.e) / math.sqrt(D)
CHUNKS = ((0, 2), (2, 2), (4, 2))
BF = jnp.bfloat16
F32 = jnp.float32


ANY = pl.BlockSpec(memory_space=pl.ANY)
SMEM = pl.BlockSpec(memory_space=pltpu.SMEM)
VMEM = pl.BlockSpec(memory_space=pltpu.VMEM)


def copies(plan, count, outs, name, scalars, arrays):
    def body(scalar_ref, *refs):
        ins, rest = refs[: len(arrays)], refs[len(arrays) :]
        dst, sems = rest[:-1], rest[-1]
        moves = [
            pltpu.make_async_copy(a, b, sems.at[i]) for i, (a, b) in enumerate(plan(scalar_ref, ins, dst))
        ]
        for move in moves:
            move.start()
        for move in moves:
            move.wait()

    return pl.pallas_call(
        body,
        in_specs=[SMEM] + [ANY] * len(arrays),
        out_specs=[ANY] * len(outs),
        out_shape=outs,
        scratch_shapes=[pltpu.SemaphoreType.DMA((count,))],
        name=name,
    )(scalars, *arrays)


def column(head):
    return pl.ds(pl.multiple_of(head * D, D), D)


def pack(arrays, first, heads, rows, name, peers):
    def plan(peer, ins, outs):
        return [
            (ins[a].at[:, column(peer[d] * HD + first + h)], outs[d].at[a, h])
            for d in range(GROUP)
            for a in range(len(arrays))
            for h in range(heads)
        ]

    outs = [jax.ShapeDtypeStruct((len(arrays), heads, rows, D), BF)] * GROUP
    return copies(plan, GROUP * len(arrays) * heads, outs, name, peers, arrays)


def join_slice(pieces, heads, peers):
    def plan(_, ins, outs):
        return [(ins[d], outs[0].at[:, :, pl.ds(d * ROWS, ROWS), :]) for d in range(GROUP)]

    outs = [jax.ShapeDtypeStruct((2, heads, SLICE, D), BF)]
    return copies(plan, GROUP, outs, "join_slice", peers, pieces)[0]


def unpack(chunks, sources):
    flat = [piece for chunk in chunks for piece in chunk]

    def plan(src, ins, outs):
        moves = []
        for c, (first, heads) in enumerate(CHUNKS):
            for d in range(GROUP):
                for h in range(heads):
                    moves.append((ins[c * GROUP + d].at[h], outs[0].at[:, column(src[d] * HD + first + h)]))
        return moves

    outs = [jax.ShapeDtypeStruct((ROWS, HEADS * D), BF)]
    return copies(plan, HEADS, outs, "unpack", sources, flat)[0]


def around(block, axis, distance):
    return lax.ppermute(block, axis, [(i, (i + distance) % GROUP) for i in range(GROUP)])


def exchange(pieces):
    return [pieces[0]] + [around(pieces[d], "uly", d) for d in range(1, GROUP)]


def beside(block, distance):
    return lax.ppermute(block, "blk", [(i, i + distance) for i in range(BLK) if 0 <= i + distance < BLK])


def text_body(src, t0, t1, t2, t3, kv, bias, o_ref, lse_ref, q_sc, k_sc, v_sc):
    for d, t in enumerate((t0, t1, t2, t3)):
        q_sc[pl.ds(pl.multiple_of(src[d] * TROWS, TROWS), TROWS), :] = t[0, 0]
        k_sc[SLICE + d * TROWS : SLICE + (d + 1) * TROWS, :] = t[1, 0]
        v_sc[SLICE + d * TROWS : SLICE + (d + 1) * TROWS, :] = t[2, 0]
    k_sc[:SLICE, :] = kv[0, 0]
    v_sc[:SLICE, :] = kv[1, 0]
    s = lax.dot_general(q_sc[...], k_sc[...], (((1,), (1,)), ((), ())), preferred_element_type=F32)
    s = jnp.concatenate([s[:, :SLICE], s[:, SLICE:] + bias[...]], axis=1)
    top = jnp.max(s, axis=1, keepdims=True)
    p = jnp.exp2(s * SCALE - top * SCALE)
    total = jnp.sum(p, axis=1, keepdims=True)
    o = jnp.dot(p.astype(BF), v_sc[...], preferred_element_type=F32) / total
    o_ref[0] = o
    lse_ref[0] = jnp.broadcast_to(top * SCALE + jnp.log2(total), (TXT, D))


def text_attention(sources, text, first, heads, kv, bias):
    piece = pl.BlockSpec((3, 1, TROWS, D), lambda h: (0, first + h, 0, 0))
    return pl.pallas_call(
        text_body,
        grid=(heads,),
        in_specs=[SMEM]
        + [piece] * GROUP
        + [pl.BlockSpec((2, 1, SLICE, D), lambda h: (0, h, 0, 0)), pl.BlockSpec((1, TXT), lambda h: (0, 0))],
        out_specs=[pl.BlockSpec((1, TXT, D), lambda h: (h, 0, 0))] * 2,
        out_shape=[jax.ShapeDtypeStruct((heads, TXT, D), F32)] * 2,
        scratch_shapes=[
            pltpu.VMEM((TXT, D), BF),
            pltpu.VMEM((SLICE + TXT, D), BF),
            pltpu.VMEM((SLICE + TXT, D), BF),
        ],
        name="text_attention",
    )(sources, *text, kv, bias)


SLOT = 16
PAIRS = 12


def spread_body(*refs):
    n = len(CHUNKS)
    o_refs, lse_refs, out_ref, sc = refs[:n], refs[n : 2 * n], refs[2 * n], refs[2 * n + 1]
    sc[...] = jnp.zeros_like(sc)
    lane = lax.broadcasted_iota(jnp.int32, (TROWS, D), 1)
    where = [(c, h) for c, (_, heads) in enumerate(CHUNKS) for h in range(heads)]
    for p in range(2):
        logs = jnp.zeros((TROWS, D), F32)
        for u2 in range(GROUP):
            for i in range(3):
                c, h = where[3 * p + i]
                s = 3 * u2 + i
                rows = pl.ds(u2 * TROWS, TROWS)
                sc[pl.ds(SLOT * p + s, TROWS, stride=2 * SLOT), :] = o_refs[c][h, rows, :]
                logs = jnp.where(lane == s, lse_refs[c][h, rows, :], logs)
        for part in range(3):
            rounded = logs.astype(BF).astype(F32)
            sc[pl.ds(SLOT * p + PAIRS + part, TROWS, stride=2 * SLOT), :] = rounded
            logs = logs - rounded
    out_ref[...] = sc[...].astype(BF).reshape(DEVS, SLOT, D)


def spread(o, lse):
    return pl.pallas_call(
        spread_body,
        in_specs=[VMEM] * (2 * len(CHUNKS)),
        out_specs=VMEM,
        out_shape=jax.ShapeDtypeStruct((DEVS, SLOT, D), BF),
        scratch_shapes=[pltpu.VMEM((DEVS * SLOT, D), F32)],
        name="spread",
    )(*o, *lse)


def combine_body(in_ref, out_ref, sc, res):
    sc[...] = in_ref[...].astype(F32).reshape(DEVS * SLOT, D)
    logs = sc[pl.ds(PAIRS, DEVS, stride=SLOT), :]
    for part in range(1, 3):
        logs = logs + sc[pl.ds(PAIRS + part, DEVS, stride=SLOT), :]
    logs = jnp.transpose(logs)[:SLOT]
    group = lax.broadcasted_iota(jnp.int32, (SLOT, DEVS), 1) % GROUP
    top = jnp.zeros((SLOT, DEVS), F32)
    for u in range(GROUP):
        best = jnp.max(jnp.where(group == u, logs, -jnp.inf), axis=1, keepdims=True)
        top = jnp.where(group == u, best, top)
    weights = jnp.exp2(logs - top)
    total = jnp.ones((SLOT, DEVS), F32)
    for u in range(GROUP):
        all_u = jnp.sum(jnp.where(group == u, weights, 0.0), axis=1, keepdims=True)
        total = jnp.where(group == u, all_u, total)
    weights = weights / total
    mine = lax.broadcasted_iota(jnp.int32, (8, DEVS), 1) % GROUP == lax.broadcasted_iota(jnp.int32, (8, DEVS), 0)
    res[...] = jnp.zeros_like(res)
    for u2 in range(GROUP):
        for i in range(3):
            s = 3 * u2 + i
            left = jnp.where(mine, jnp.broadcast_to(weights[s : s + 1], (8, DEVS)), 0.0)
            values = sc[pl.ds(s, DEVS, stride=SLOT), :]
            got = jnp.dot(left, values, preferred_element_type=F32, precision=lax.Precision.HIGHEST)
            for u in range(GROUP):
                res[u2, pl.ds(3 * u + i, 1), :] = got[u : u + 1]
    done = res[...].astype(BF)
    for b in range(BLK):
        out_ref[b] = done


def combine(received):
    return pl.pallas_call(
        combine_body,
        in_specs=[VMEM],
        out_specs=VMEM,
        out_shape=jax.ShapeDtypeStruct((BLK, GROUP, SLOT, D), BF),
        scratch_shapes=[pltpu.VMEM((DEVS * SLOT, D), F32), pltpu.VMEM((GROUP, SLOT, D), F32)],
        name="combine",
    )(received).reshape(DEVS, SLOT, D)


def text_rows_body(in_ref, out_ref, sc):
    sc[...] = in_ref[...].astype(F32).reshape(DEVS * SLOT, D)
    for p in range(2):
        for u in range(GROUP):
            for i in range(3):
                rows = sc[pl.ds(SLOT * p + 3 * u + i, TROWS, stride=2 * SLOT), :]
                head = HD * u + 3 * p + i
                out_ref[:, head * D : (head + 1) * D] = rows.astype(BF)


def text_rows(received):
    return pl.pallas_call(
        text_rows_body,
        in_specs=[VMEM],
        out_specs=VMEM,
        out_shape=jax.ShapeDtypeStruct((TROWS, HEADS * D), BF),
        scratch_shapes=[pltpu.VMEM((DEVS * SLOT, D), F32)],
        name="text_rows",
    )(received)


def video_body(first, heads, scalars, *refs):
    q_refs, refs = refs[:GROUP], refs[GROUP:]
    text, refs = refs[:GROUP], refs[GROUP:]
    before, own, after, bias, refs = refs[0], refs[1], refs[2], refs[3], refs[4:]
    o_refs, refs = refs[:GROUP], refs[GROUP:]
    q_sc, k_sc, v_sc, o_sc, sem, o_sem = refs

    def loads(h):
        moves = []
        for d in range(GROUP):
            rows = pl.ds(pl.multiple_of(scalars[d] * ROWS, 32), ROWS)
            moves.append((q_refs[d].at[0, h], q_sc.at[h, rows]))
        for a, sc in ((0, k_sc), (1, v_sc)):
            moves.append((before.at[a, h], sc.at[h, pl.ds(0, SLICE)]))
            moves.append((own.at[a, h], sc.at[h, pl.ds(SLICE, SLICE)]))
            for d in range(GROUP):
                rows = pl.ds(2 * SLICE + d * TROWS, TROWS)
                moves.append((text[d].at[1 + a, first + h], sc.at[h, rows]))
            moves.append((after.at[a, h], sc.at[h, pl.ds(KEYS, SLICE)]))
        return [pltpu.make_async_copy(a, b, sem.at[h, i]) for i, (a, b) in enumerate(moves)]

    def stores(h):
        moves = []
        for d in range(GROUP):
            rows = pl.ds(pl.multiple_of(scalars[GROUP + d] * ROWS, 32), ROWS)
            moves.append(pltpu.make_async_copy(o_sc.at[h, rows], o_refs[d].at[h], o_sem.at[h, d]))
        return moves

    for h in range(heads):
        for move in loads(h):
            move.start()

    def side(i):
        return scalars[2 * GROUP + i * RB // TILE]

    def scores(h, i):
        keys = k_sc[h, pl.ds(pl.multiple_of(side(i) * SLICE, RB), KEYS), :]
        return lax.dot_general(
            q_sc[h, i * RB : (i + 1) * RB, :], keys, (((1,), (1,)), ((), ())), preferred_element_type=F32
        )

    def finish(h, i, s):
        f = side(i)
        s = jnp.concatenate(
            [
                s[:, :SLICE],
                s[:, SLICE : SLICE + TXT] + bias[f, 0:1, :],
                s[:, SLICE + TXT : 2 * SLICE],
                s[:, 2 * SLICE :] + bias[f, 1:2, :],
            ],
            axis=1,
        )
        top = jnp.max(s, axis=1, keepdims=True)
        p = jnp.exp2(s * SCALE - top * SCALE)
        total = jnp.sum(p, axis=1, keepdims=True)
        values = v_sc[h, pl.ds(pl.multiple_of(f * SLICE, RB), KEYS), :]
        o = jnp.dot(p.astype(BF), values, preferred_element_type=F32)
        o_sc[h, i * RB : (i + 1) * RB, :] = (o / total).astype(BF)

    steps = SLICE // RB
    for h in range(heads):
        for move in loads(h):
            move.wait()
        s = scores(h, 0)
        for i in range(steps):
            following = scores(h, i + 1) if i + 1 < steps else None
            finish(h, i, s)
            s = following
        for move in stores(h):
            move.start()
    for h in range(heads):
        for move in stores(h):
            move.wait()


def video_attention(first, heads, scalars, q, text, before, own, after, bias):
    return pl.pallas_call(
        functools.partial(video_body, first, heads),
        in_specs=[SMEM] + [ANY] * (2 * GROUP + 3) + [VMEM],
        out_specs=[ANY] * GROUP,
        out_shape=[jax.ShapeDtypeStruct((heads, ROWS, D), BF)] * GROUP,
        scratch_shapes=[
            pltpu.VMEM((heads, SLICE, D), BF),
            pltpu.VMEM((heads, KEYS + SLICE, D), BF),
            pltpu.VMEM((heads, KEYS + SLICE, D), BF),
            pltpu.VMEM((heads, SLICE, D), BF),
            pltpu.SemaphoreType.DMA((heads, 18)),
            pltpu.SemaphoreType.DMA((heads, GROUP)),
        ],
        name="video_attention",
    )(scalars, *q, *text, before, own, after, bias)


def local(video_q, video_k, video_v, text_q, text_k, text_v, window_tiles, text_len):
    u, b = lax.axis_index("uly"), lax.axis_index("blk")
    steps = jnp.arange(GROUP, dtype=jnp.int32)
    targets = (u + steps) % GROUP
    sources = (u - steps) % GROUP
    text_per_slice = window_tiles.shape[0]
    side = jnp.any(window_tiles // text_per_slice > b, axis=1).astype(jnp.int32)
    scalars = jnp.concatenate([sources, targets, side]).astype(jnp.int32)
    position = (sources[:, None] * TROWS + jnp.arange(TROWS, dtype=jnp.int32)[None, :]).reshape(1, TXT)
    live = position < text_len[0]
    bias = jnp.where(live, 0.0, -jnp.inf).astype(F32)
    none = jnp.zeros_like(bias)
    video_bias = jnp.stack([jnp.concatenate([none, bias]), jnp.concatenate([bias, none])])
    text_bias = jnp.where(live & (b == 0), 0.0, -jnp.inf).astype(F32)

    kv_out, q_out = [], []
    text_out = pack((text_q, text_k, text_v), 0, HD, TROWS, "pack_text", targets)
    for first, heads in CHUNKS:
        kv_out.append(pack((video_k, video_v), first, heads, ROWS, "pack_kv", targets))
        q_out.append(pack((video_q,), first, heads, ROWS, "pack_q", targets))
    text = exchange(text_out)
    own, before, after, q = [], [], [], []
    for c, (first, heads) in enumerate(CHUNKS):
        own.append(join_slice(exchange(kv_out[c]), heads, targets))
        before.append(beside(own[c], 1))
        after.append(beside(own[c], -1))
        q.append(exchange(q_out[c]))
    parts = [text_attention(sources, text, f, n, own[c], text_bias) for c, (f, n) in enumerate(CHUNKS)]
    slots = spread([p[0] for p in parts], [p[1] for p in parts])
    slots = lax.all_to_all(slots, ("blk", "uly"), 0, 0, tiled=True)
    slots = lax.all_to_all(combine(slots), ("blk", "uly"), 0, 0, tiled=True)
    text_result = text_rows(slots)
    back = []
    for c, (first, heads) in enumerate(CHUNKS):
        o = video_attention(first, heads, scalars, q[c], text, before[c], own[c], after[c], video_bias)
        back.append(exchange(o))
    return unpack(back, sources), text_result


def solution(mesh):
    in_specs = (
        P(("blk", "uly"), None),
        P(("blk", "uly"), None),
        P(("blk", "uly"), None),
        P("uly", None),
        P("uly", None),
        P("uly", None),
        P("blk", None),
        P(),
    )
    out_specs = (P(("blk", "uly"), None), P("uly", None))
    return jax.shard_map(local, mesh=mesh, in_specs=in_specs, out_specs=out_specs, check_vma=False)
```

```python
import functools
import math

import jax
import jax.numpy as jnp
from jax import lax
from jax.experimental import pallas as pl
from jax.experimental.pallas import tpu as pltpu
from jax.sharding import PartitionSpec as P


HEADS = 24
D = 128
TXT = 256
GROUP = 4
HD = HEADS // GROUP
ROWS = 288
SLICE = ROWS * GROUP
TILE = 384
TROWS = TXT // GROUP
BLK = 32
DEVS = GROUP * BLK
RB = 128
KEYS = 2 * SLICE + TXT
SCALE = math.log2(math.e) / math.sqrt(D)
CHUNKS = ((0, 3), (3, 3))
BF = jnp.bfloat16
F32 = jnp.float32


HBM = pl.BlockSpec(memory_space=pltpu.HBM)
SMEM = pl.BlockSpec(memory_space=pltpu.SMEM)
VMEM = pl.BlockSpec(memory_space=pltpu.VMEM)


def place(distance):
    return (lax.axis_index("uly") + distance + GROUP) % GROUP


def column(head):
    return pl.ds(pl.multiple_of(head * D, D), D)


def rows_of(position, count):
    return pl.ds(pl.multiple_of(position * count, 32), count)


def run(moves):
    for move in moves:
        move.start()


def wait(moves):
    for move in moves:
        move.wait()


def copy_list(pairs, sems):
    return [pltpu.make_async_copy(a, b, sems.at[i]) for i, (a, b) in enumerate(pairs)]


def pack(arrays, jobs):
    outs = []
    for numbers, _, heads, together in jobs:
        shape = (len(numbers), heads, arrays[numbers[0]].shape[0], D)
        if together:
            outs.append(jax.ShapeDtypeStruct((GROUP, *shape), BF))
        else:
            outs += [jax.ShapeDtypeStruct(shape, BF)] * GROUP

    def body(*refs):
        ins, rest = refs[: len(arrays)], refs[len(arrays) :]
        dst, held, in_sems, out_sems = rest[: len(outs)], rest[len(outs) : -2], rest[-2], rest[-1]
        reads, writes, n = [], [], 0
        for numbers, first, heads, together in jobs:
            for d in range(GROUP):
                group = d if together else place(d)
                here = held[n].at[d] if together else held[n]
                there = dst[n].at[d] if together else dst[n]
                pairs = [
                    (ins[k].at[:, column(group * HD + first + h)], here.at[i, h])
                    for i, k in enumerate(numbers)
                    for h in range(heads)
                ]
                base = sum(len(r) for r in reads)
                reads.append([pltpu.make_async_copy(x, y, in_sems.at[base + i]) for i, (x, y) in enumerate(pairs)])
                writes.append(pltpu.make_async_copy(here, there, out_sems.at[len(writes)]))
                n += not together
            n += together
        for read in reads:
            run(read)
        for read, write in zip(reads, writes):
            wait(read)
            write.start()
        wait(writes)

    got = pl.pallas_call(
        body,
        in_specs=[HBM] * len(arrays),
        out_specs=[HBM] * len(outs),
        out_shape=outs,
        scratch_shapes=[pltpu.VMEM(o.shape, BF) for o in outs]
        + [pltpu.SemaphoreType.DMA((160,)), pltpu.SemaphoreType.DMA((32,))],
    )(*arrays)
    result, n = [], 0
    for job in jobs:
        result.append(got[n] if job[3] else got[n : n + GROUP])
        n += 1 if job[3] else GROUP
    return result


def around(block, distance):
    return lax.ppermute(block, "uly", [(i, (i + distance) % GROUP) for i in range(GROUP)])


def exchange(pieces):
    got = [pieces[0]]
    for d in range(1, GROUP):
        got.append(around(pieces[d], d))
    return got


def swap(array, axes):
    return lax.all_to_all(array, axes, 0, 0, tiled=True)


def beside(block, distance):
    return lax.ppermute(block, "blk", [(i, i + distance) for i in range(BLK) if 0 <= i + distance < BLK])


def text_bias(length):
    lane = lax.broadcasted_iota(jnp.int32, (1, TXT), 1)
    position = (lax.axis_index("uly") + GROUP - lane // TROWS) % GROUP * TROWS + lane % TROWS
    return jnp.where(position < length, 0.0, -jnp.inf).astype(F32)


def weigh(q, keys, values, masked):
    s = lax.dot_general(q, keys(), (((1,), (1,)), ((), ())), preferred_element_type=F32)
    return s, lambda: finish(s, values, masked)


def finish(s, values, masked):
    parts, at = [], 0
    for start, bias in masked:
        parts += [s[:, at:start], s[:, start : start + TXT] + bias]
        at = start + TXT
    if at < s.shape[1]:
        parts.append(s[:, at:])
    s = jnp.concatenate([p for p in parts if p.shape[1]], axis=1)
    top = jnp.max(s, axis=1, keepdims=True)
    p = jnp.exp2(s * SCALE - top * SCALE)
    total = jnp.sum(p, axis=1, keepdims=True)
    o = jnp.dot(p.astype(BF), values(), preferred_element_type=F32)
    return o / total, top * SCALE + jnp.log2(total)


SLOT = 16
PAIRS = 12


def text_body(length, *refs):
    text, kv, refs = refs[:GROUP], refs[GROUP : GROUP + len(CHUNKS)], refs[GROUP + len(CHUNKS) :]
    out_ref, q_sc, kv_sc, o_sc, log_sc, sc, slots, sems = refs
    pairs = []
    for d in range(GROUP):
        pairs.append((text[d].at[0], q_sc.at[:, rows_of(place(-d), TROWS)]))
        pairs.append((text[d].at[pl.ds(1, 2)], kv_sc.at[:, :, pl.ds(SLICE + d * TROWS, TROWS)]))
    for c, (first, heads) in enumerate(CHUNKS):
        for g in range(GROUP):
            pairs.append((kv[c].at[g], kv_sc.at[:, pl.ds(first, heads), pl.ds(g * ROWS, ROWS)]))
    moves = copy_list(pairs, sems)
    run(moves)
    sc[...] = jnp.zeros_like(sc)
    bias = jnp.where(lax.axis_index("blk") == 0, text_bias(length[0]), -jnp.inf)
    wait(moves)
    steps = [(h, i) for h in range(HD) for i in range(TXT // RB)]

    def begin(h, i):
        q = q_sc[h, i * RB : (i + 1) * RB]
        return weigh(q, lambda: kv_sc[0, h], lambda: kv_sc[1, h], [(SLICE, bias)])[1]

    rest = begin(*steps[0])
    for n, (h, i) in enumerate(steps):
        following = begin(*steps[n + 1]) if n + 1 < len(steps) else None
        o, log = rest()
        o_sc[h, i * RB : (i + 1) * RB] = o
        log_sc[h, i * RB : (i + 1) * RB] = jnp.broadcast_to(log, (RB, D))
        rest = following
    lane = lax.broadcasted_iota(jnp.int32, (TROWS, D), 1)
    for p in range(2):
        logs = jnp.zeros((TROWS, D), F32)
        for u2 in range(GROUP):
            rows = pl.ds(u2 * TROWS, TROWS)
            for i in range(3):
                s = 3 * u2 + i
                sc[pl.ds(SLOT * p + s, TROWS, stride=2 * SLOT), :] = o_sc[3 * p + i, rows, :]
                logs = jnp.where(lane == s, log_sc[3 * p + i, rows, :], logs)
        for part in range(3):
            rounded = logs.astype(BF).astype(F32)
            sc[pl.ds(SLOT * p + PAIRS + part, TROWS, stride=2 * SLOT), :] = rounded
            logs = logs - rounded
    slots[...] = sc[...].astype(BF).reshape(DEVS, SLOT, D)
    leave(slots, out_ref, sems)


def leave(held, out_ref, sems):
    size = held.shape[0] // 4
    parts = [pl.ds(i * size, size) for i in range(4)]
    moves = copy_list([(held.at[x], out_ref.at[x]) for x in parts], sems)
    run(moves)
    wait(moves)


def text_attention(length, text, kv):
    return pl.pallas_call(
        text_body,
        in_specs=[SMEM] + [HBM] * (GROUP + len(CHUNKS)),
        out_specs=HBM,
        out_shape=jax.ShapeDtypeStruct((DEVS, SLOT, D), BF),
        scratch_shapes=[
            pltpu.VMEM((HD, TXT, D), BF),
            pltpu.VMEM((2, HD, SLICE + TXT, D), BF),
            pltpu.VMEM((HD, TXT, D), F32),
            pltpu.VMEM((HD, TXT, D), F32),
            pltpu.VMEM((DEVS * SLOT, D), F32),
            pltpu.VMEM((DEVS, SLOT, D), BF),
            pltpu.SemaphoreType.DMA((32,)),
        ],
        name="text_attention",
    )(length, *text, *kv)


def combine_body(in_ref, out_ref, sc, res, slots, sems):
    sc[...] = in_ref[...].astype(F32).reshape(DEVS * SLOT, D)
    logs = sc[pl.ds(PAIRS, DEVS, stride=SLOT), :]
    for part in range(1, 3):
        logs = logs + sc[pl.ds(PAIRS + part, DEVS, stride=SLOT), :]
    logs = jnp.transpose(logs)[:SLOT]
    group = lax.broadcasted_iota(jnp.int32, (SLOT, DEVS), 1) % GROUP
    top = jnp.zeros((SLOT, DEVS), F32)
    for u in range(GROUP):
        best = jnp.max(jnp.where(group == u, logs, -jnp.inf), axis=1, keepdims=True)
        top = jnp.where(group == u, best, top)
    weights = jnp.exp2(logs - top)
    total = jnp.ones((SLOT, DEVS), F32)
    for u in range(GROUP):
        all_u = jnp.sum(jnp.where(group == u, weights, 0.0), axis=1, keepdims=True)
        total = jnp.where(group == u, all_u, total)
    weights = weights / total
    mine = lax.broadcasted_iota(jnp.int32, (8, DEVS), 1) % GROUP == lax.broadcasted_iota(jnp.int32, (8, DEVS), 0)
    res[...] = jnp.zeros_like(res)
    for u2 in range(GROUP):
        for i in range(3):
            s = 3 * u2 + i
            left = jnp.where(mine, jnp.broadcast_to(weights[s : s + 1], (8, DEVS)), 0.0)
            values = sc[pl.ds(s, DEVS, stride=SLOT), :]
            got = jnp.dot(left, values, preferred_element_type=F32, precision=lax.Precision.HIGHEST)
            for u in range(GROUP):
                res[u2, pl.ds(3 * u + i, 1), :] = got[u : u + 1]
    done = res[...].astype(BF)
    for b in range(BLK):
        slots[b] = done
    leave(slots, out_ref, sems)


def combine(received):
    return pl.pallas_call(
        combine_body,
        in_specs=[VMEM],
        out_specs=HBM,
        out_shape=jax.ShapeDtypeStruct((BLK, GROUP, SLOT, D), BF),
        scratch_shapes=[
            pltpu.VMEM((DEVS * SLOT, D), F32),
            pltpu.VMEM((GROUP, SLOT, D), F32),
            pltpu.VMEM((BLK, GROUP, SLOT, D), BF),
            pltpu.SemaphoreType.DMA((4,)),
        ],
        name="combine",
    )(received).reshape(DEVS, SLOT, D)


def video_body(first, heads, tiles, length, *refs):
    q_refs, text, refs = refs[:GROUP], refs[GROUP : 2 * GROUP], refs[2 * GROUP :]
    before, own, after, refs = refs[0], refs[1], refs[2], refs[3:]
    o_refs, refs = refs[:GROUP], refs[GROUP:]
    q_sc, k_sc, v_sc, o_sc, side_sc, sems, o_sems = refs

    def loads(start, count, slot):
        some = pl.ds(start, count)
        parts = []
        for a, sc in ((0, k_sc), (1, v_sc)):
            pairs = []
            for base, kv in ((0, before), (SLICE, own), (KEYS, after)):
                for g in range(GROUP):
                    pairs.append((kv.at[g, a, some], sc.at[some, pl.ds(base + g * ROWS, ROWS)]))
            for d in range(GROUP):
                rows = pl.ds(2 * SLICE + d * TROWS, TROWS)
                pairs.append((text[d].at[1 + a, pl.ds(first + start, count)], sc.at[some, rows]))
            parts.append(pairs)
        queries = [(q_refs[d].at[0, some], q_sc.at[some, rows_of(place(-d), ROWS)]) for d in range(GROUP)]
        pairs = queries + parts[0] + parts[1]
        return copy_list(pairs, sems.at[slot]), len(queries + parts[0])

    def stores(h):
        return [
            pltpu.make_async_copy(o_sc.at[h, rows_of(place(d), ROWS)], o_refs[d].at[h], o_sems.at[h, d])
            for d in range(GROUP)
        ]

    head, keys_only = loads(0, 1, 0)
    others, _ = loads(1, heads - 1, 1)
    run(head)
    run(others)
    limit = (lax.axis_index("blk") + 1) * tiles.shape[0]
    for j in range(tiles.shape[0]):
        last = tiles[j, 0]
        for w in range(1, tiles.shape[1]):
            last = jnp.maximum(last, tiles[j, w])
        side_sc[j] = (last >= limit).astype(jnp.int32)
    live = text_bias(length[0])

    def step(h, i):
        f = side_sc[i * RB // TILE]
        window = pl.ds(pl.multiple_of(f * SLICE, RB), KEYS)
        masked = [(SLICE, jnp.where(f == 1, live, 0.0)), (2 * SLICE, jnp.where(f == 1, 0.0, live))]
        q = q_sc[h, i * RB : (i + 1) * RB, :]
        return weigh(q, lambda: k_sc[h, window], lambda: v_sc[h, window], masked)[1]

    steps = SLICE // RB
    wait(head[:keys_only])

    def one(h, _):
        @pl.when(h == 1)
        def _():
            wait(others)

        rest = step(h, 0)

        @pl.when(h == 0)
        def _():
            wait(head[keys_only:])

        for i in range(steps):
            following = step(h, i + 1) if i + 1 < steps else None
            o, _ = rest()
            o_sc[h, i * RB : (i + 1) * RB, :] = o.astype(BF)
            rest = following
        run(stores(h))
        return 0

    lax.fori_loop(0, heads, one, 0)
    for h in range(heads):
        wait(stores(h))


def video_attention(first, heads, tiles, length, q, text, before, own, after):
    return pl.pallas_call(
        functools.partial(video_body, first, heads),
        in_specs=[SMEM, SMEM] + [HBM] * (2 * GROUP + 3),
        out_specs=[HBM] * GROUP,
        out_shape=[jax.ShapeDtypeStruct((heads, ROWS, D), BF)] * GROUP,
        scratch_shapes=[
            pltpu.VMEM((heads, SLICE, D), BF),
            pltpu.VMEM((heads, KEYS + SLICE, D), BF),
            pltpu.VMEM((heads, KEYS + SLICE, D), BF),
            pltpu.VMEM((heads, SLICE, D), BF),
            pltpu.SMEM((8,), jnp.int32),
            pltpu.SemaphoreType.DMA((2, 40)),
            pltpu.SemaphoreType.DMA((heads, GROUP)),
        ],
        name="video_attention",
    )(tiles, length, *q, *text, before, own, after)


SLABS = 6


def rows_body(*refs):
    count = len(CHUNKS) * GROUP
    pieces, slots, video_out, text_out, held, sc, in_sems, out_sems = (refs[:count], *refs[count:])
    pairs = []
    for c, (first, heads) in enumerate(CHUNKS):
        for d in range(GROUP):
            for h in range(heads):
                pairs.append((pieces[c * GROUP + d].at[h], held.at[:, column(place(-d) * HD + first + h)]))
    reads = copy_list(pairs, in_sems)
    run(reads)
    wait(reads)
    size = ROWS // SLABS
    slabs = [pl.ds(i * size, size) for i in range(SLABS)]
    writes = copy_list([(held.at[x], video_out.at[x]) for x in slabs], out_sems)
    run(writes)
    sc[...] = slots[...].astype(F32).reshape(DEVS * SLOT, D)
    for p in range(2):
        for u in range(GROUP):
            for i in range(3):
                rows = sc[pl.ds(SLOT * p + 3 * u + i, TROWS, stride=2 * SLOT), :]
                head = HD * u + 3 * p + i
                text_out[:, head * D : (head + 1) * D] = rows.astype(BF)
    wait(writes)


def side_by_side(chunks, slots):
    flat = [piece for chunk in chunks for piece in chunk]
    return pl.pallas_call(
        rows_body,
        in_specs=[HBM] * len(flat) + [VMEM],
        out_specs=[HBM, VMEM],
        out_shape=[
            jax.ShapeDtypeStruct((ROWS, HEADS * D), BF),
            jax.ShapeDtypeStruct((TROWS, HEADS * D), BF),
        ],
        scratch_shapes=[
            pltpu.VMEM((ROWS, HEADS * D), BF),
            pltpu.VMEM((DEVS * SLOT, D), F32),
            pltpu.SemaphoreType.DMA((HEADS,)),
            pltpu.SemaphoreType.DMA((SLABS,)),
        ],
        name="side_by_side",
    )(*flat, slots)


def local(video_q, video_k, video_v, text_q, text_k, text_v, window_tiles, text_len):
    video, words = (video_q, video_k, video_v), (text_q, text_k, text_v)
    (f0, n0), (f1, n1) = CHUNKS
    (kv0,) = pack(video, [((1, 2), f0, n0, True)])
    text, q0, kv1, q1 = pack(
        video + words, [((3, 4, 5), 0, HD, False), ((0,), f0, n0, False), ((1, 2), f1, n1, True), ((0,), f1, n1, False)]
    )
    own, before, after = [], [], []
    for kv in (kv0, kv1):
        own.append(swap(kv, "uly"))
        before.append(beside(own[-1], 1))
        after.append(beside(own[-1], -1))
    text = exchange(text)
    q = [exchange(q0), exchange(q1)]
    slots = text_attention(text_len, text, own)
    slots = swap(slots, ("blk", "uly"))
    slots = combine(slots)
    slots = swap(slots, ("blk", "uly"))
    back = []
    for c, (first, heads) in enumerate(CHUNKS):
        o = video_attention(first, heads, window_tiles, text_len, q[c], text, before[c], own[c], after[c])
        back.append(exchange(o))
    return side_by_side(back, slots)


def solution(mesh):
    in_specs = (
        P(("blk", "uly"), None),
        P(("blk", "uly"), None),
        P(("blk", "uly"), None),
        P("uly", None),
        P("uly", None),
        P("uly", None),
        P("blk", None),
        P(),
    )
    out_specs = (P(("blk", "uly"), None), P("uly", None))

    return jax.shard_map(local, mesh=mesh, in_specs=in_specs, out_specs=out_specs, check_vma=False)
```

```python
import functools
import math

import jax
import jax.numpy as jnp
from jax import lax
from jax.experimental import pallas as pl
from jax.experimental.pallas import tpu as pltpu
from jax.sharding import PartitionSpec as P


HEADS = 24
D = 128
TXT = 256
GROUP = 4
HD = HEADS // GROUP
ROWS = 288
SLICE = ROWS * GROUP
TILE = 384
TROWS = TXT // GROUP
HALF = TROWS // 2
BLK = 32
DEVS = GROUP * BLK
RB = 128
KEYS = 2 * SLICE + TXT
SCALE = math.log2(math.e) / math.sqrt(D)
CHUNKS = ((0, 2), (2, 4))
BF = jnp.bfloat16
F32 = jnp.float32


HBM = pl.BlockSpec(memory_space=pltpu.HBM)
SMEM = pl.BlockSpec(memory_space=pltpu.SMEM)
VMEM = pl.BlockSpec(memory_space=pltpu.VMEM)


def place(distance):
    return (lax.axis_index("uly") + distance + GROUP) % GROUP


def half(which):
    return (lax.axis_index("blk") + which) % 2


def column(head):
    return pl.ds(pl.multiple_of(head * D, D), D)


def rows_of(position, count):
    return pl.ds(pl.multiple_of(position * count, 32), count)


def run(moves):
    for move in moves:
        move.start()


def wait(moves):
    for move in moves:
        move.wait()


def copy_list(pairs, sems):
    return [pltpu.make_async_copy(a, b, sems.at[i]) for i, (a, b) in enumerate(pairs)]


def pack(arrays, jobs):
    outs = []
    for numbers, _, heads, rows, together in jobs:
        shape = (len(numbers), heads, rows, D)
        if together:
            outs.append(jax.ShapeDtypeStruct((GROUP, *shape), BF))
        else:
            outs += [jax.ShapeDtypeStruct(shape, BF)] * (GROUP + (rows == HALF))

    def body(*refs):
        ins, rest = refs[: len(arrays)], refs[len(arrays) :]
        dst, held, in_sems, out_sems = rest[: len(outs)], rest[len(outs) : -2], rest[-2], rest[-1]
        reads, writes, n = [], [], 0
        for numbers, first, heads, rows, together in jobs:
            for d in range(GROUP + (rows == HALF)):
                which = slice(None) if rows == ROWS else rows_of(half(d // GROUP), rows)
                group = d if together else place(d % GROUP)
                here = held[n].at[d] if together else held[n]
                there = dst[n].at[d] if together else dst[n]
                pairs = [
                    (ins[k].at[which, column(group * HD + first + h)], here.at[i, h])
                    for i, k in enumerate(numbers)
                    for h in range(heads)
                ]
                base = sum(len(r) for r in reads)
                reads.append([pltpu.make_async_copy(x, y, in_sems.at[base + i]) for i, (x, y) in enumerate(pairs)])
                writes.append(pltpu.make_async_copy(here, there, out_sems.at[len(writes)]))
                n += not together
            n += together
        for read in reads:
            run(read)
        for read, write in zip(reads, writes):
            wait(read)
            write.start()
        wait(writes)

    got = pl.pallas_call(
        body,
        in_specs=[HBM] * len(arrays),
        out_specs=[HBM] * len(outs),
        out_shape=outs,
        scratch_shapes=[pltpu.VMEM(o.shape, BF) for o in outs]
        + [pltpu.SemaphoreType.DMA((160,)), pltpu.SemaphoreType.DMA((32,))],
    )(*arrays)
    result, n = [], 0
    for job in jobs:
        count = 1 if job[4] else GROUP + (job[3] == HALF)
        result.append(got[n] if job[4] else got[n : n + count])
        n += count
    return result


def around(block, distance):
    return lax.ppermute(block, "uly", [(i, (i + distance) % GROUP) for i in range(GROUP)])


def exchange(pieces):
    got = [pieces[0]]
    for d in range(1, GROUP):
        got.append(around(pieces[d], d))
    return got


def swap(array, axes):
    return lax.all_to_all(array, axes, 0, 0, tiled=True)


def beside(block, distance):
    return lax.ppermute(block, "blk", [(i, i + distance) for i in range(BLK) if 0 <= i + distance < BLK])


def text_bias(length):
    lane = lax.broadcasted_iota(jnp.int32, (1, TXT), 1)
    which = (lane // (TXT // 2) + half(0)) % 2
    source = (lax.axis_index("uly") + GROUP - lane % (TXT // 2) // HALF) % GROUP
    position = source * TROWS + which * HALF + lane % HALF
    return jnp.where(position < length, 0.0, -jnp.inf).astype(F32)


def weigh(q, keys, values, masked):
    s = lax.dot_general(q, keys(), (((1,), (1,)), ((), ())), preferred_element_type=F32)
    return s, lambda: finish(s, values, masked)


def finish(s, values, masked):
    parts, at = [], 0
    for start, bias in masked:
        parts += [s[:, at:start], s[:, start : start + TXT] + bias]
        at = start + TXT
    if at < s.shape[1]:
        parts.append(s[:, at:])
    s = jnp.concatenate([p for p in parts if p.shape[1]], axis=1)
    top = jnp.max(s, axis=1, keepdims=True)
    p = jnp.exp2(s * SCALE - top * SCALE)
    total = jnp.sum(p, axis=1, keepdims=True)
    o = jnp.dot(p.astype(BF), values(), preferred_element_type=F32)
    return o / total, top * SCALE + jnp.log2(total)


SLOT = 16
PAIRS = 12


def text_body(length, *refs):
    text, kv, refs = refs[: 2 * GROUP], refs[2 * GROUP :][: len(CHUNKS)], refs[2 * GROUP + len(CHUNKS) :]
    out_ref, q_sc, kv_sc, o_sc, log_sc, sc, slots, sems = refs
    pairs = []
    for n, piece in enumerate(text):
        pairs.append((piece.at[0], q_sc.at[:, rows_of(2 * place(-(n % GROUP)) + half(n // GROUP), HALF)]))
        pairs.append((piece.at[pl.ds(1, 2)], kv_sc.at[:, :, pl.ds(SLICE + n * HALF, HALF)]))
    for c, (first, heads) in enumerate(CHUNKS):
        for g in range(GROUP):
            pairs.append((kv[c].at[g], kv_sc.at[:, pl.ds(first, heads), pl.ds(g * ROWS, ROWS)]))
    moves = copy_list(pairs, sems)
    run(moves)
    sc[...] = jnp.zeros_like(sc)
    bias = jnp.where(lax.axis_index("blk") == 0, text_bias(length[0]), -jnp.inf)
    wait(moves)
    steps = [(h, i) for h in range(HD) for i in range(TXT // RB)]

    def begin(h, i):
        q = q_sc[h, i * RB : (i + 1) * RB]
        return weigh(q, lambda: kv_sc[0, h], lambda: kv_sc[1, h], [(SLICE, bias)])[1]

    rest = begin(*steps[0])
    for n, (h, i) in enumerate(steps):
        following = begin(*steps[n + 1]) if n + 1 < len(steps) else None
        o, log = rest()
        o_sc[h, i * RB : (i + 1) * RB] = o
        log_sc[h, i * RB : (i + 1) * RB] = jnp.broadcast_to(log, (RB, D))
        rest = following
    lane = lax.broadcasted_iota(jnp.int32, (TROWS, D), 1)
    for p in range(2):
        logs = jnp.zeros((TROWS, D), F32)
        for u2 in range(GROUP):
            rows = pl.ds(u2 * TROWS, TROWS)
            for i in range(3):
                s = 3 * u2 + i
                sc[pl.ds(SLOT * p + s, TROWS, stride=2 * SLOT), :] = o_sc[3 * p + i, rows, :]
                logs = jnp.where(lane == s, log_sc[3 * p + i, rows, :], logs)
        for part in range(3):
            rounded = logs.astype(BF).astype(F32)
            sc[pl.ds(SLOT * p + PAIRS + part, TROWS, stride=2 * SLOT), :] = rounded
            logs = logs - rounded
    slots[...] = sc[...].astype(BF).reshape(DEVS, SLOT, D)
    leave(slots, out_ref, sems)


def leave(held, out_ref, sems):
    size = held.shape[0] // 4
    parts = [pl.ds(i * size, size) for i in range(4)]
    moves = copy_list([(held.at[x], out_ref.at[x]) for x in parts], sems)
    run(moves)
    wait(moves)


def text_attention(length, text, kv):
    return pl.pallas_call(
        text_body,
        in_specs=[SMEM] + [HBM] * (2 * GROUP + len(CHUNKS)),
        out_specs=HBM,
        out_shape=jax.ShapeDtypeStruct((DEVS, SLOT, D), BF),
        scratch_shapes=[
            pltpu.VMEM((HD, TXT, D), BF),
            pltpu.VMEM((2, HD, SLICE + TXT, D), BF),
            pltpu.VMEM((HD, TXT, D), F32),
            pltpu.VMEM((HD, TXT, D), F32),
            pltpu.VMEM((DEVS * SLOT, D), F32),
            pltpu.VMEM((DEVS, SLOT, D), BF),
            pltpu.SemaphoreType.DMA((32,)),
        ],
        name="text_attention",
    )(length, *text, *kv)


def combine_body(in_ref, out_ref, sc, res, slots, sems):
    sc[...] = in_ref[...].astype(F32).reshape(DEVS * SLOT, D)
    logs = sc[pl.ds(PAIRS, DEVS, stride=SLOT), :]
    for part in range(1, 3):
        logs = logs + sc[pl.ds(PAIRS + part, DEVS, stride=SLOT), :]
    logs = jnp.transpose(logs)[:SLOT]
    group = lax.broadcasted_iota(jnp.int32, (SLOT, DEVS), 1) % GROUP
    top = jnp.zeros((SLOT, DEVS), F32)
    for u in range(GROUP):
        best = jnp.max(jnp.where(group == u, logs, -jnp.inf), axis=1, keepdims=True)
        top = jnp.where(group == u, best, top)
    weights = jnp.exp2(logs - top)
    total = jnp.ones((SLOT, DEVS), F32)
    for u in range(GROUP):
        all_u = jnp.sum(jnp.where(group == u, weights, 0.0), axis=1, keepdims=True)
        total = jnp.where(group == u, all_u, total)
    weights = weights / total
    mine = lax.broadcasted_iota(jnp.int32, (8, DEVS), 1) % GROUP == lax.broadcasted_iota(jnp.int32, (8, DEVS), 0)
    res[...] = jnp.zeros_like(res)
    for u2 in range(GROUP):
        for i in range(3):
            s = 3 * u2 + i
            left = jnp.where(mine, jnp.broadcast_to(weights[s : s + 1], (8, DEVS)), 0.0)
            values = sc[pl.ds(s, DEVS, stride=SLOT), :]
            got = jnp.dot(left, values, preferred_element_type=F32, precision=lax.Precision.HIGHEST)
            for u in range(GROUP):
                res[u2, pl.ds(3 * u + i, 1), :] = got[u : u + 1]
    done = res[...].astype(BF)
    for b in range(BLK):
        slots[b] = done
    leave(slots, out_ref, sems)


def combine(received):
    return pl.pallas_call(
        combine_body,
        in_specs=[VMEM],
        out_specs=HBM,
        out_shape=jax.ShapeDtypeStruct((BLK, GROUP, SLOT, D), BF),
        scratch_shapes=[
            pltpu.VMEM((DEVS * SLOT, D), F32),
            pltpu.VMEM((GROUP, SLOT, D), F32),
            pltpu.VMEM((BLK, GROUP, SLOT, D), BF),
            pltpu.SemaphoreType.DMA((4,)),
        ],
        name="combine",
    )(received).reshape(DEVS, SLOT, D)


def video_body(first, heads, tiles, length, *refs):
    q_refs, text, refs = refs[:GROUP], refs[GROUP : 3 * GROUP], refs[3 * GROUP :]
    before, own, after, refs = refs[0], refs[1], refs[2], refs[3:]
    o_refs, refs = refs[:GROUP], refs[GROUP:]
    q_sc, k_sc, v_sc, o_sc, side_sc, sems, o_sems = refs

    def loads(start, count, slot):
        some = pl.ds(start, count)
        parts = []
        for a, sc in ((0, k_sc), (1, v_sc)):
            pairs = []
            for base, kv in ((0, before), (SLICE, own), (KEYS, after)):
                for g in range(GROUP):
                    pairs.append((kv.at[g, a, some], sc.at[some, pl.ds(base + g * ROWS, ROWS)]))
            for n, piece in enumerate(text):
                rows = pl.ds(2 * SLICE + n * HALF, HALF)
                pairs.append((piece.at[1 + a, pl.ds(first + start, count)], sc.at[some, rows]))
            parts.append(pairs)
        queries = [(q_refs[d].at[0, some], q_sc.at[some, rows_of(place(-d), ROWS)]) for d in range(GROUP)]
        pairs = queries + parts[0] + parts[1]
        return copy_list(pairs, sems.at[slot]), len(queries + parts[0])

    def stores(h):
        return [
            pltpu.make_async_copy(o_sc.at[h, rows_of(place(d), ROWS)], o_refs[d].at[h], o_sems.at[h, d])
            for d in range(GROUP)
        ]

    head, keys_only = loads(0, 1, 0)
    others, _ = loads(1, heads - 1, 1)
    run(head)
    run(others)
    limit = (lax.axis_index("blk") + 1) * tiles.shape[0]
    for j in range(tiles.shape[0]):
        last = tiles[j, 0]
        for w in range(1, tiles.shape[1]):
            last = jnp.maximum(last, tiles[j, w])
        side_sc[j] = (last >= limit).astype(jnp.int32)
    live = text_bias(length[0])

    def step(h, i):
        f = side_sc[i * RB // TILE]
        window = pl.ds(pl.multiple_of(f * SLICE, RB), KEYS)
        masked = [(SLICE, jnp.where(f == 1, live, 0.0)), (2 * SLICE, jnp.where(f == 1, 0.0, live))]
        q = q_sc[h, i * RB : (i + 1) * RB, :]
        return weigh(q, lambda: k_sc[h, window], lambda: v_sc[h, window], masked)[1]

    steps = SLICE // RB
    wait(head[:keys_only])

    def one(h, _):
        @pl.when(h == 1)
        def _():
            wait(others)

        rest = step(h, 0)

        @pl.when(h == 0)
        def _():
            wait(head[keys_only:])

        for i in range(steps):
            following = step(h, i + 1) if i + 1 < steps else None
            o, _ = rest()
            o_sc[h, i * RB : (i + 1) * RB, :] = o.astype(BF)
            rest = following
        run(stores(h))
        return 0

    lax.fori_loop(0, heads, one, 0)
    for h in range(heads):
        wait(stores(h))


def video_attention(first, heads, tiles, length, q, text, before, own, after):
    return pl.pallas_call(
        functools.partial(video_body, first, heads),
        in_specs=[SMEM, SMEM] + [HBM] * (3 * GROUP + 3),
        out_specs=[HBM] * GROUP,
        out_shape=[jax.ShapeDtypeStruct((heads, ROWS, D), BF)] * GROUP,
        scratch_shapes=[
            pltpu.VMEM((heads, SLICE, D), BF),
            pltpu.VMEM((heads, KEYS + SLICE, D), BF),
            pltpu.VMEM((heads, KEYS + SLICE, D), BF),
            pltpu.VMEM((heads, SLICE, D), BF),
            pltpu.SMEM((8,), jnp.int32),
            pltpu.SemaphoreType.DMA((2, 48)),
            pltpu.SemaphoreType.DMA((heads, GROUP)),
        ],
        name="video_attention",
    )(tiles, length, *q, *text, before, own, after)


def rows_body(first, heads, *refs):
    pieces, refs = refs[:GROUP], refs[-4:]
    video_out, held, in_sems, out_sems = refs
    reads, writes = [], []
    for d in range(GROUP):
        for h in range(heads):
            n = len(reads)
            reads.append(pltpu.make_async_copy(pieces[d].at[h], held.at[n], in_sems.at[n]))
            there = video_out.at[:, column(place(-d) * HD + first + h)]
            writes.append(pltpu.make_async_copy(held.at[n], there, out_sems.at[n]))
    run(reads)
    for read, write in zip(reads, writes):
        read.wait()
        write.start()
    return writes


def first_body(first, heads, *refs):
    pieces, slots, video_out, text_out, held, sc, in_sems, out_sems = refs[:GROUP], *refs[GROUP:]
    writes = rows_body(first, heads, *pieces, video_out, held, in_sems, out_sems)
    sc[...] = slots[...].astype(F32).reshape(DEVS * SLOT, D)
    for p in range(2):
        for u in range(GROUP):
            for i in range(3):
                rows = sc[pl.ds(SLOT * p + 3 * u + i, TROWS, stride=2 * SLOT), :]
                head = HD * u + 3 * p + i
                text_out[:, head * D : (head + 1) * D] = rows.astype(BF)
    wait(writes)


def later_body(first, heads, *refs):
    wait(rows_body(first, heads, *refs))


def first_rows(pieces, slots, first, heads):
    return pl.pallas_call(
        functools.partial(first_body, first, heads),
        in_specs=[HBM] * GROUP + [VMEM],
        out_specs=[HBM, VMEM],
        out_shape=[
            jax.ShapeDtypeStruct((ROWS, HEADS * D), BF),
            jax.ShapeDtypeStruct((TROWS, HEADS * D), BF),
        ],
        scratch_shapes=[
            pltpu.VMEM((GROUP * heads, ROWS, D), BF),
            pltpu.VMEM((DEVS * SLOT, D), F32),
            pltpu.SemaphoreType.DMA((GROUP * heads,)),
            pltpu.SemaphoreType.DMA((GROUP * heads,)),
        ],
        name="first_rows",
    )(*pieces, slots)


def later_rows(pieces, rows, first, heads):
    return pl.pallas_call(
        functools.partial(later_body, first, heads),
        in_specs=[HBM] * (GROUP + 1),
        out_specs=HBM,
        out_shape=jax.ShapeDtypeStruct((ROWS, HEADS * D), BF),
        scratch_shapes=[
            pltpu.VMEM((GROUP * heads, ROWS, D), BF),
            pltpu.SemaphoreType.DMA((GROUP * heads,)),
            pltpu.SemaphoreType.DMA((GROUP * heads,)),
        ],
        input_output_aliases={GROUP: 0},
        name="later_rows",
    )(*pieces, rows)


def local(video_q, video_k, video_v, text_q, text_k, text_v, window_tiles, text_len):
    video, words = (video_q, video_k, video_v), (text_q, text_k, text_v)
    (f0, n0), (f1, n1) = CHUNKS
    (kv0,) = pack(video, [((1, 2), f0, n0, ROWS, True)])
    q0, text, kv1, q1 = pack(
        video + words,
        [
            ((0,), f0, n0, ROWS, False),
            ((3, 4, 5), 0, HD, HALF, False),
            ((1, 2), f1, n1, ROWS, True),
            ((0,), f1, n1, ROWS, False),
        ],
    )
    own, before, after = [], [], []
    for kv in (kv0, kv1):
        own.append(swap(kv, "uly"))
        before.append(beside(own[-1], 1))
        after.append(beside(own[-1], -1))
    mine = exchange(text[:GROUP])
    other = [text[GROUP]]
    for d in range(1, GROUP):
        other.append(lax.ppermute(mine[d], "blk", [(i, i ^ 1) for i in range(BLK)]))
    text = mine + other
    q = [exchange(q0), exchange(q1)]
    slots = text_attention(text_len, text, own)
    slots = swap(slots, ("blk", "uly"))
    slots = combine(slots)
    slots = swap(slots, ("blk", "uly"))
    back = []
    for c, (first, heads) in enumerate(CHUNKS):
        o = video_attention(first, heads, window_tiles, text_len, q[c], text, before[c], own[c], after[c])
        back.append(exchange(o))
    rows, text_out = first_rows(back[0], slots, f0, n0)
    return later_rows(back[1], rows, f1, n1), text_out


def solution(mesh):
    in_specs = (
        P(("blk", "uly"), None),
        P(("blk", "uly"), None),
        P(("blk", "uly"), None),
        P("uly", None),
        P("uly", None),
        P("uly", None),
        P("blk", None),
        P(),
    )
    out_specs = (P(("blk", "uly"), None), P("uly", None))

    return jax.shard_map(local, mesh=mesh, in_specs=in_specs, out_specs=out_specs, check_vma=False)
```

```python
import functools
import math

import jax
import jax.numpy as jnp
from jax import lax
from jax.experimental import pallas as pl
from jax.experimental.pallas import tpu as pltpu
from jax.sharding import PartitionSpec as P


HEADS = 24
D = 128
TXT = 256
GROUP = 4
HD = HEADS // GROUP
ROWS = 288
SLICE = ROWS * GROUP
TILE = 384
TROWS = TXT // GROUP
HALF = TROWS // 2
BLK = 32
DEVS = GROUP * BLK
RB = 128
KEYS = 2 * SLICE + TXT
SCALE = math.log2(math.e) / math.sqrt(D)
CHUNKS = ((0, 4), (4, 2))
BF = jnp.bfloat16
F32 = jnp.float32


HBM = pl.BlockSpec(memory_space=pltpu.HBM)
SMEM = pl.BlockSpec(memory_space=pltpu.SMEM)
VMEM = pl.BlockSpec(memory_space=pltpu.VMEM)


def place(distance):
    return (lax.axis_index("uly") + distance + GROUP) % GROUP


def half(which):
    return (lax.axis_index("blk") + which) % 2


def column(head):
    return pl.ds(pl.multiple_of(head * D, D), D)


def rows_of(position, count):
    return pl.ds(pl.multiple_of(position * count, 32), count)


def run(moves):
    for move in moves:
        move.start()


def wait(moves):
    for move in moves:
        move.wait()


def copy_list(pairs, sems):
    return [pltpu.make_async_copy(a, b, sems.at[i]) for i, (a, b) in enumerate(pairs)]


def pack(arrays, jobs):
    outs = []
    for numbers, _, heads, rows, together in jobs:
        shape = (len(numbers), heads, rows, D)
        if together:
            outs.append(jax.ShapeDtypeStruct((GROUP, *shape), BF))
        else:
            outs += [jax.ShapeDtypeStruct(shape, BF)] * (GROUP + (rows == HALF))

    def body(*refs):
        ins, rest = refs[: len(arrays)], refs[len(arrays) :]
        dst, held, in_sems, out_sems = rest[: len(outs)], rest[len(outs) : -2], rest[-2], rest[-1]
        reads, writes, n = [], [], 0
        for numbers, first, heads, rows, together in jobs:
            for d in range(GROUP + (rows == HALF)):
                which = slice(None) if rows == ROWS else rows_of(half(d // GROUP), rows)
                group = d if together else place(d % GROUP)
                here = held[n].at[d] if together else held[n]
                there = dst[n].at[d] if together else dst[n]
                pairs = [
                    (ins[k].at[which, column(group * HD + first + h)], here.at[i, h])
                    for i, k in enumerate(numbers)
                    for h in range(heads)
                ]
                base = sum(len(r) for r in reads)
                reads.append([pltpu.make_async_copy(x, y, in_sems.at[base + i]) for i, (x, y) in enumerate(pairs)])
                writes.append(pltpu.make_async_copy(here, there, out_sems.at[len(writes)]))
                n += not together
            n += together
        for read in reads:
            run(read)
        for read, write in zip(reads, writes):
            wait(read)
            write.start()
        wait(writes)

    got = pl.pallas_call(
        body,
        in_specs=[HBM] * len(arrays),
        out_specs=[HBM] * len(outs),
        out_shape=outs,
        scratch_shapes=[pltpu.VMEM(o.shape, BF) for o in outs]
        + [pltpu.SemaphoreType.DMA((160,)), pltpu.SemaphoreType.DMA((32,))],
    )(*arrays)
    result, n = [], 0
    for job in jobs:
        count = 1 if job[4] else GROUP + (job[3] == HALF)
        result.append(got[n] if job[4] else got[n : n + count])
        n += count
    return result


def around(block, distance):
    return lax.ppermute(block, "uly", [(i, (i + distance) % GROUP) for i in range(GROUP)])


def exchange(pieces):
    got = [pieces[0]]
    for d in range(1, GROUP):
        got.append(around(pieces[d], d))
    return got


def swap(array, axes):
    return lax.all_to_all(array, axes, 0, 0, tiled=True)


def beside(block, distance):
    return lax.ppermute(block, "blk", [(i, i + distance) for i in range(BLK) if 0 <= i + distance < BLK])


def text_bias(length):
    lane = lax.broadcasted_iota(jnp.int32, (1, TXT), 1)
    which = (lane // (TXT // 2) + half(0)) % 2
    source = (lax.axis_index("uly") + GROUP - lane % (TXT // 2) // HALF) % GROUP
    position = source * TROWS + which * HALF + lane % HALF
    return jnp.where(position < length, 0.0, -jnp.inf).astype(F32)


def weigh(q, keys, values, masked):
    s = lax.dot_general(q, keys(), (((1,), (1,)), ((), ())), preferred_element_type=F32)
    return s, lambda: finish(s, values, masked)


def finish(s, values, masked):
    parts, at = [], 0
    for start, bias in masked:
        parts += [s[:, at:start], s[:, start : start + TXT] + bias]
        at = start + TXT
    if at < s.shape[1]:
        parts.append(s[:, at:])
    s = jnp.concatenate([p for p in parts if p.shape[1]], axis=1)
    top = jnp.max(s, axis=1, keepdims=True)
    p = jnp.exp2(s * SCALE - top * SCALE)
    total = jnp.sum(p, axis=1, keepdims=True)
    o = jnp.dot(p.astype(BF), values(), preferred_element_type=F32)
    return o / total, top * SCALE + jnp.log2(total)


SLOT = 16
PAIRS = 12


def text_body(length, *refs):
    text, kv, refs = refs[: 2 * GROUP], refs[2 * GROUP :][: len(CHUNKS)], refs[2 * GROUP + len(CHUNKS) :]
    out_ref, q_sc, kv_sc, o_sc, log_sc, sc, slots, sems = refs
    pairs = []
    for n, piece in enumerate(text):
        pairs.append((piece.at[0], q_sc.at[:, rows_of(2 * place(-(n % GROUP)) + half(n // GROUP), HALF)]))
        pairs.append((piece.at[pl.ds(1, 2)], kv_sc.at[:, :, pl.ds(SLICE + n * HALF, HALF)]))
    for c, (first, heads) in enumerate(CHUNKS):
        for g in range(GROUP):
            pairs.append((kv[c].at[g], kv_sc.at[:, pl.ds(first, heads), pl.ds(g * ROWS, ROWS)]))
    moves = copy_list(pairs, sems)
    run(moves)
    sc[...] = jnp.zeros_like(sc)
    bias = jnp.where(lax.axis_index("blk") == 0, text_bias(length[0]), -jnp.inf)
    wait(moves)
    steps = [(h, i) for h in range(HD) for i in range(TXT // RB)]

    def begin(h, i):
        q = q_sc[h, i * RB : (i + 1) * RB]
        return weigh(q, lambda: kv_sc[0, h], lambda: kv_sc[1, h], [(SLICE, bias)])[1]

    rest = begin(*steps[0])
    for n, (h, i) in enumerate(steps):
        following = begin(*steps[n + 1]) if n + 1 < len(steps) else None
        o, log = rest()
        o_sc[h, i * RB : (i + 1) * RB] = o
        log_sc[h, i * RB : (i + 1) * RB] = jnp.broadcast_to(log, (RB, D))
        rest = following
    lane = lax.broadcasted_iota(jnp.int32, (TROWS, D), 1)
    for p in range(2):
        logs = jnp.zeros((TROWS, D), F32)
        for u2 in range(GROUP):
            rows = pl.ds(u2 * TROWS, TROWS)
            for i in range(3):
                s = 3 * u2 + i
                sc[pl.ds(SLOT * p + s, TROWS, stride=2 * SLOT), :] = o_sc[3 * p + i, rows, :]
                logs = jnp.where(lane == s, log_sc[3 * p + i, rows, :], logs)
        for part in range(3):
            rounded = logs.astype(BF).astype(F32)
            sc[pl.ds(SLOT * p + PAIRS + part, TROWS, stride=2 * SLOT), :] = rounded
            logs = logs - rounded
    slots[...] = sc[...].astype(BF).reshape(DEVS, SLOT, D)
    leave(slots, out_ref, sems)


def leave(held, out_ref, sems):
    size = held.shape[0] // 4
    parts = [pl.ds(i * size, size) for i in range(4)]
    moves = copy_list([(held.at[x], out_ref.at[x]) for x in parts], sems)
    run(moves)
    wait(moves)


def text_attention(length, text, kv):
    return pl.pallas_call(
        text_body,
        in_specs=[SMEM] + [HBM] * (2 * GROUP + len(CHUNKS)),
        out_specs=HBM,
        out_shape=jax.ShapeDtypeStruct((DEVS, SLOT, D), BF),
        scratch_shapes=[
            pltpu.VMEM((HD, TXT, D), BF),
            pltpu.VMEM((2, HD, SLICE + TXT, D), BF),
            pltpu.VMEM((HD, TXT, D), F32),
            pltpu.VMEM((HD, TXT, D), F32),
            pltpu.VMEM((DEVS * SLOT, D), F32),
            pltpu.VMEM((DEVS, SLOT, D), BF),
            pltpu.SemaphoreType.DMA((32,)),
        ],
        name="text_attention",
    )(length, *text, *kv)


def combine_body(in_ref, out_ref, sc, res, slots, sems):
    sc[...] = in_ref[...].astype(F32).reshape(DEVS * SLOT, D)
    logs = sc[pl.ds(PAIRS, DEVS, stride=SLOT), :]
    for part in range(1, 3):
        logs = logs + sc[pl.ds(PAIRS + part, DEVS, stride=SLOT), :]
    logs = jnp.transpose(logs)[:SLOT]
    group = lax.broadcasted_iota(jnp.int32, (SLOT, DEVS), 1) % GROUP
    top = jnp.zeros((SLOT, DEVS), F32)
    for u in range(GROUP):
        best = jnp.max(jnp.where(group == u, logs, -jnp.inf), axis=1, keepdims=True)
        top = jnp.where(group == u, best, top)
    weights = jnp.exp2(logs - top)
    total = jnp.ones((SLOT, DEVS), F32)
    for u in range(GROUP):
        all_u = jnp.sum(jnp.where(group == u, weights, 0.0), axis=1, keepdims=True)
        total = jnp.where(group == u, all_u, total)
    weights = weights / total
    mine = lax.broadcasted_iota(jnp.int32, (8, DEVS), 1) % GROUP == lax.broadcasted_iota(jnp.int32, (8, DEVS), 0)
    res[...] = jnp.zeros_like(res)
    for u2 in range(GROUP):
        for i in range(3):
            s = 3 * u2 + i
            left = jnp.where(mine, jnp.broadcast_to(weights[s : s + 1], (8, DEVS)), 0.0)
            values = sc[pl.ds(s, DEVS, stride=SLOT), :]
            got = jnp.dot(left, values, preferred_element_type=F32, precision=lax.Precision.HIGHEST)
            for u in range(GROUP):
                res[u2, pl.ds(3 * u + i, 1), :] = got[u : u + 1]
    done = res[...].astype(BF)
    for b in range(BLK):
        slots[b] = done
    leave(slots, out_ref, sems)


def combine(received):
    return pl.pallas_call(
        combine_body,
        in_specs=[VMEM],
        out_specs=HBM,
        out_shape=jax.ShapeDtypeStruct((BLK, GROUP, SLOT, D), BF),
        scratch_shapes=[
            pltpu.VMEM((DEVS * SLOT, D), F32),
            pltpu.VMEM((GROUP, SLOT, D), F32),
            pltpu.VMEM((BLK, GROUP, SLOT, D), BF),
            pltpu.SemaphoreType.DMA((4,)),
        ],
        name="combine",
    )(received).reshape(DEVS, SLOT, D)


def video_body(first, heads, tiles, length, *refs):
    q_refs, text, refs = refs[:GROUP], refs[GROUP : 3 * GROUP], refs[3 * GROUP :]
    before, own, after, refs = refs[0], refs[1], refs[2], refs[3:]
    o_refs, refs = refs[:GROUP], refs[GROUP:]
    q_sc, k_sc, v_sc, o_sc, side_sc, sems, o_sems = refs

    def loads(start, count, slot):
        some = pl.ds(start, count)
        parts = []
        for a, sc in ((0, k_sc), (1, v_sc)):
            pairs = []
            for base, kv in ((0, before), (SLICE, own), (KEYS, after)):
                for g in range(GROUP):
                    pairs.append((kv.at[g, a, some], sc.at[some, pl.ds(base + g * ROWS, ROWS)]))
            for n, piece in enumerate(text):
                rows = pl.ds(2 * SLICE + n * HALF, HALF)
                pairs.append((piece.at[1 + a, pl.ds(first + start, count)], sc.at[some, rows]))
            parts.append(pairs)
        asked = pl.ds(first + start, count)
        queries = [(q_refs[d].at[0, asked], q_sc.at[some, rows_of(place(-d), ROWS)]) for d in range(GROUP)]
        pairs = queries + parts[0] + parts[1]
        return copy_list(pairs, sems.at[slot]), len(queries + parts[0])

    def stores(h):
        return [
            pltpu.make_async_copy(o_sc.at[h, rows_of(place(d), ROWS)], o_refs[d].at[h], o_sems.at[h, d])
            for d in range(GROUP)
        ]

    head, keys_only = loads(0, 1, 0)
    others, _ = loads(1, heads - 1, 1)
    run(head)
    run(others)
    limit = (lax.axis_index("blk") + 1) * tiles.shape[0]
    for j in range(tiles.shape[0]):
        last = tiles[j, 0]
        for w in range(1, tiles.shape[1]):
            last = jnp.maximum(last, tiles[j, w])
        side_sc[j] = (last >= limit).astype(jnp.int32)
    live = text_bias(length[0])

    def step(h, i):
        f = side_sc[i * RB // TILE]
        window = pl.ds(pl.multiple_of(f * SLICE, RB), KEYS)
        masked = [(SLICE, jnp.where(f == 1, live, 0.0)), (2 * SLICE, jnp.where(f == 1, 0.0, live))]
        q = q_sc[h, i * RB : (i + 1) * RB, :]
        return weigh(q, lambda: k_sc[h, window], lambda: v_sc[h, window], masked)[1]

    steps = SLICE // RB
    wait(head[:keys_only])

    def one(h, _):
        @pl.when(h == 1)
        def _():
            wait(others)

        rest = step(h, 0)

        @pl.when(h == 0)
        def _():
            wait(head[keys_only:])

        for i in range(steps):
            following = step(h, i + 1) if i + 1 < steps else None
            o, _ = rest()
            o_sc[h, i * RB : (i + 1) * RB, :] = o.astype(BF)
            rest = following
        run(stores(h))
        return 0

    lax.fori_loop(0, heads, one, 0)
    for h in range(heads):
        wait(stores(h))


def video_attention(first, heads, tiles, length, q, text, before, own, after):
    return pl.pallas_call(
        functools.partial(video_body, first, heads),
        in_specs=[SMEM, SMEM] + [HBM] * (3 * GROUP + 3),
        out_specs=[HBM] * GROUP,
        out_shape=[jax.ShapeDtypeStruct((heads, ROWS, D), BF)] * GROUP,
        scratch_shapes=[
            pltpu.VMEM((heads, SLICE, D), BF),
            pltpu.VMEM((heads, KEYS + SLICE, D), BF),
            pltpu.VMEM((heads, KEYS + SLICE, D), BF),
            pltpu.VMEM((heads, SLICE, D), BF),
            pltpu.SMEM((8,), jnp.int32),
            pltpu.SemaphoreType.DMA((2, 48)),
            pltpu.SemaphoreType.DMA((heads, GROUP)),
        ],
        name="video_attention",
    )(tiles, length, *q, *text, before, own, after)


def rows_body(first, heads, *refs):
    pieces, refs = refs[:GROUP], refs[-4:]
    video_out, held, in_sems, out_sems = refs
    reads, writes = [], []
    for d in range(GROUP):
        for h in range(heads):
            n = len(reads)
            reads.append(pltpu.make_async_copy(pieces[d].at[h], held.at[n], in_sems.at[n]))
            there = video_out.at[:, column(place(-d) * HD + first + h)]
            writes.append(pltpu.make_async_copy(held.at[n], there, out_sems.at[n]))
    run(reads)
    for read, write in zip(reads, writes):
        read.wait()
        write.start()
    return writes


def first_body(first, heads, *refs):
    pieces, slots, video_out, text_out, held, sc, in_sems, out_sems = refs[:GROUP], *refs[GROUP:]
    writes = rows_body(first, heads, *pieces, video_out, held, in_sems, out_sems)
    sc[...] = slots[...].astype(F32).reshape(DEVS * SLOT, D)
    for p in range(2):
        for u in range(GROUP):
            for i in range(3):
                rows = sc[pl.ds(SLOT * p + 3 * u + i, TROWS, stride=2 * SLOT), :]
                head = HD * u + 3 * p + i
                text_out[:, head * D : (head + 1) * D] = rows.astype(BF)
    wait(writes)


def later_body(first, heads, *refs):
    wait(rows_body(first, heads, *refs))


def first_rows(pieces, slots, first, heads):
    return pl.pallas_call(
        functools.partial(first_body, first, heads),
        in_specs=[HBM] * GROUP + [VMEM],
        out_specs=[HBM, VMEM],
        out_shape=[
            jax.ShapeDtypeStruct((ROWS, HEADS * D), BF),
            jax.ShapeDtypeStruct((TROWS, HEADS * D), BF),
        ],
        scratch_shapes=[
            pltpu.VMEM((GROUP * heads, ROWS, D), BF),
            pltpu.VMEM((DEVS * SLOT, D), F32),
            pltpu.SemaphoreType.DMA((GROUP * heads,)),
            pltpu.SemaphoreType.DMA((GROUP * heads,)),
        ],
        name="first_rows",
    )(*pieces, slots)


def later_rows(pieces, rows, first, heads):
    return pl.pallas_call(
        functools.partial(later_body, first, heads),
        in_specs=[HBM] * (GROUP + 1),
        out_specs=HBM,
        out_shape=jax.ShapeDtypeStruct((ROWS, HEADS * D), BF),
        scratch_shapes=[
            pltpu.VMEM((GROUP * heads, ROWS, D), BF),
            pltpu.SemaphoreType.DMA((GROUP * heads,)),
            pltpu.SemaphoreType.DMA((GROUP * heads,)),
        ],
        input_output_aliases={GROUP: 0},
        name="later_rows",
    )(*pieces, rows)


def local(video_q, video_k, video_v, text_q, text_k, text_v, window_tiles, text_len):
    video, words = (video_q, video_k, video_v), (text_q, text_k, text_v)
    (f0, n0), (f1, n1) = CHUNKS
    (kv0,) = pack(video, [((1, 2), f0, n0, ROWS, True)])
    text, kv1, q = pack(
        video + words,
        [
            ((3, 4, 5), 0, HD, HALF, False),
            ((1, 2), f1, n1, ROWS, True),
            ((0,), 0, HD, ROWS, False),
        ],
    )
    own, before, after = [], [], []
    for kv in (kv0, kv1):
        own.append(swap(kv, "uly"))
        before.append(beside(own[-1], 1))
        after.append(beside(own[-1], -1))
    mine = exchange(text[:GROUP])
    other = [text[GROUP]]
    for d in range(1, GROUP):
        other.append(lax.ppermute(mine[d], "blk", [(i, i ^ 1) for i in range(BLK)]))
    text = mine + other
    q = exchange(q)
    slots = text_attention(text_len, text, own)
    slots = swap(slots, ("blk", "uly"))
    slots = combine(slots)
    slots = swap(slots, ("blk", "uly"))
    back = []
    for c, (first, heads) in enumerate(CHUNKS):
        o = video_attention(first, heads, window_tiles, text_len, q, text, before[c], own[c], after[c])
        back.append(exchange(o))
    rows, text_out = first_rows(back[0], slots, f0, n0)
    return later_rows(back[1], rows, f1, n1), text_out


def solution(mesh):
    in_specs = (
        P(("blk", "uly"), None),
        P(("blk", "uly"), None),
        P(("blk", "uly"), None),
        P("uly", None),
        P("uly", None),
        P("uly", None),
        P("blk", None),
        P(),
    )
    out_specs = (P(("blk", "uly"), None), P("uly", None))

    return jax.shard_map(local, mesh=mesh, in_specs=in_specs, out_specs=out_specs, check_vma=False)
```

```python
import functools
import math

import jax
import jax.numpy as jnp
from jax import lax
from jax.experimental import pallas as pl
from jax.experimental.pallas import tpu as pltpu
from jax.sharding import PartitionSpec as P


HEADS = 24
D = 128
TXT = 256
GROUP = 4
HD = HEADS // GROUP
ROWS = 288
SLICE = ROWS * GROUP
TILE = 384
TROWS = TXT // GROUP
HALF = TROWS // 2
BLK = 32
DEVS = GROUP * BLK
RB = 128
SCALE = math.log2(math.e) / math.sqrt(D)
CHUNKS = ((0, 4), (4, 2))
LIMIT = 67043328
BF = jnp.bfloat16
F32 = jnp.float32


ANY = pl.BlockSpec(memory_space=pl.ANY)
PARAMS = pltpu.CompilerParams(vmem_limit_bytes=LIMIT)
SMEM = pl.BlockSpec(memory_space=pltpu.SMEM)
VMEM = pl.BlockSpec(memory_space=pltpu.VMEM)


def place(distance):
    return (lax.axis_index("uly") + distance + GROUP) % GROUP


def half(which):
    return (lax.axis_index("blk") + which) % 2


def column(head):
    return pl.ds(pl.multiple_of(head * D, D), D)


def rows_of(position, count):
    return pl.ds(pl.multiple_of(position * count, 32), count)


def run(moves):
    for move in moves:
        move.start()


def wait(moves):
    for move in moves:
        move.wait()


def copy_list(pairs, sems):
    return [pltpu.make_async_copy(a, b, sems.at[i]) for i, (a, b) in enumerate(pairs)]


def pack(arrays, jobs):
    outs = []
    for numbers, _, heads, rows, together in jobs:
        shape = (len(numbers), heads, rows, D)
        if together:
            outs.append(jax.ShapeDtypeStruct((GROUP, *shape), BF))
        else:
            outs += [jax.ShapeDtypeStruct(shape, BF)] * (GROUP + (rows == HALF))

    def body(*refs):
        ins, rest = refs[: len(arrays)], refs[len(arrays) :]
        dst, held, in_sems, out_sems = rest[: len(outs)], rest[len(outs) : -2], rest[-2], rest[-1]
        reads, writes, n = [], [], 0
        for numbers, first, heads, rows, together in jobs:
            for d in range(GROUP + (rows == HALF)):
                which = slice(None) if rows == ROWS else rows_of(half(d // GROUP), rows)
                group = d if together else place(d % GROUP)
                here = held[n].at[d] if together else held[n]
                there = dst[n].at[d] if together else dst[n]
                pairs = [
                    (ins[k].at[which, column(group * HD + first + h)], here.at[i, h])
                    for i, k in enumerate(numbers)
                    for h in range(heads)
                ]
                base = sum(len(r) for r in reads)
                reads.append([pltpu.make_async_copy(x, y, in_sems.at[base + i]) for i, (x, y) in enumerate(pairs)])
                writes.append(pltpu.make_async_copy(here, there, out_sems.at[len(writes)]))
                n += not together
            n += together
        for read in reads:
            run(read)
        for read, write in zip(reads, writes):
            wait(read)
            write.start()
        wait(writes)

    got = pl.pallas_call(
        body,
        in_specs=[ANY] * len(arrays),
        out_specs=[ANY] * len(outs),
        out_shape=outs,
        scratch_shapes=[pltpu.VMEM(o.shape, BF) for o in outs]
        + [pltpu.SemaphoreType.DMA((160,)), pltpu.SemaphoreType.DMA((32,))],
        compiler_params=PARAMS,
    )(*arrays)
    result, n = [], 0
    for job in jobs:
        count = 1 if job[4] else GROUP + (job[3] == HALF)
        result.append(got[n] if job[4] else got[n : n + count])
        n += count
    return result


def around(block, distance):
    return lax.ppermute(block, "uly", [(i, (i + distance) % GROUP) for i in range(GROUP)])


def exchange(pieces):
    got = [pieces[0]]
    for d in range(1, GROUP):
        got.append(around(pieces[d], d))
    return got


def swap(array, axes):
    return lax.all_to_all(array, axes, 0, 0, tiled=True)


def beside(block, distance):
    return lax.ppermute(block, "blk", [(i, i + distance) for i in range(BLK) if 0 <= i + distance < BLK])


def text_bias(length):
    lane = lax.broadcasted_iota(jnp.int32, (1, TXT), 1)
    which = (lane // (TXT // 2) + half(0)) % 2
    source = (lax.axis_index("uly") + GROUP - lane % (TXT // 2) // HALF) % GROUP
    position = source * TROWS + which * HALF + lane % HALF
    return jnp.where(position < length, 0.0, -jnp.inf).astype(F32)


def weigh(q, keys, values, text_keys, text_values, bias):
    along = (((1,), (1,)), ((), ()))
    s = lax.dot_general(q, keys(), along, preferred_element_type=F32)
    t = lax.dot_general(q, text_keys(), along, preferred_element_type=F32)

    def finish():
        masked = t + bias
        top = jnp.maximum(jnp.max(s, axis=1, keepdims=True), jnp.max(masked, axis=1, keepdims=True)) * SCALE
        p = jnp.exp2(s * SCALE - top)
        w = jnp.exp2(masked * SCALE - top)
        total = jnp.sum(p, axis=1, keepdims=True) + jnp.sum(w, axis=1, keepdims=True)
        o = jnp.dot(p.astype(BF), values(), preferred_element_type=F32)
        o = o + jnp.dot(w.astype(BF), text_values(), preferred_element_type=F32)
        return o / total, top + jnp.log2(total)

    return finish


def text_loads(text, first, heads, q_sc, t_sc):
    some, pairs = pl.ds(first, heads), []
    for n, piece in enumerate(text):
        pairs.append((piece.at[pl.ds(1, 2), some], t_sc.at[:, :, pl.ds(n * HALF, HALF)]))
        if q_sc is not None:
            rows = rows_of(2 * place(-(n % GROUP)) + half(n // GROUP), HALF)
            pairs.append((piece.at[0, some], q_sc.at[:, rows]))
    return pairs


SLOT = 16
PAIRS = 12


def text_heads(length, first, heads, text, kv, extra, q_sc, kv_sc, t_sc, sems, o_sc, log_sc):
    pairs = text_loads(text, first, heads, q_sc, t_sc)
    pairs += [(kv.at[g], kv_sc.at[:, :, pl.ds(g * ROWS, ROWS)]) for g in range(GROUP)]
    moves = copy_list(pairs + extra, sems)
    run(moves)
    bias = jnp.where(lax.axis_index("blk") == 0, text_bias(length[0]), -jnp.inf)
    wait(moves)
    steps = [(h, i) for h in range(heads) for i in range(TXT // RB)]

    def begin(h, i):
        q = q_sc[h, i * RB : (i + 1) * RB]
        return weigh(q, lambda: kv_sc[0, h], lambda: kv_sc[1, h], lambda: t_sc[0, h], lambda: t_sc[1, h], bias)

    rest = begin(*steps[0])
    for n, (h, i) in enumerate(steps):
        following = begin(*steps[n + 1]) if n + 1 < len(steps) else None
        o, log = rest()
        o_sc[first + h, i * RB : (i + 1) * RB] = o.astype(BF)
        log_sc[first + h, i * RB : (i + 1) * RB] = jnp.broadcast_to(log, (RB, D))
        rest = following


def early_body(length, *refs):
    text, kv, refs = refs[: 2 * GROUP], refs[2 * GROUP], refs[2 * GROUP + 1 :]
    o_ref, log_ref, q_sc, kv_sc, t_sc, o_sc, log_sc, sems = refs
    text_heads(length, *CHUNKS[0], text, kv, [], q_sc, kv_sc, t_sc, sems, o_sc, log_sc)
    moves = copy_list([(o_sc, o_ref), (log_sc, log_ref)], sems)
    run(moves)
    wait(moves)


def text_scratch(heads):
    return [
        pltpu.VMEM((heads, TXT, D), BF),
        pltpu.VMEM((2, heads, SLICE, D), BF),
        pltpu.VMEM((2, heads, TXT, D), BF),
    ]


def early_text(length, text, kv):
    heads = CHUNKS[0][1]
    return pl.pallas_call(
        early_body,
        in_specs=[SMEM] + [ANY] * (2 * GROUP + 1),
        out_specs=[ANY] * 2,
        out_shape=[jax.ShapeDtypeStruct((heads, TXT, D), BF), jax.ShapeDtypeStruct((heads, TXT, D), F32)],
        scratch_shapes=text_scratch(heads)
        + [
            pltpu.VMEM((heads, TXT, D), BF),
            pltpu.VMEM((heads, TXT, D), F32),
            pltpu.SemaphoreType.DMA((24,)),
        ],
        compiler_params=PARAMS,
        name="early_text",
    )(length, *text, kv)


def text_body(length, *refs):
    text, refs = refs[: 2 * GROUP], refs[2 * GROUP :]
    kv, o_in, log_in, out_ref, q_sc, kv_sc, t_sc, o_sc, log_sc, sc, slots, sems = refs
    done = pl.ds(0, CHUNKS[0][1])
    extra = [(o_in, o_sc.at[done]), (log_in, log_sc.at[done])]
    sc[...] = jnp.zeros_like(sc)
    text_heads(length, *CHUNKS[1], text, kv, extra, q_sc, kv_sc, t_sc, sems, o_sc, log_sc)
    lane = lax.broadcasted_iota(jnp.int32, (TROWS, D), 1)
    for p in range(2):
        logs = jnp.zeros((TROWS, D), F32)
        for u2 in range(GROUP):
            rows = pl.ds(u2 * TROWS, TROWS)
            for i in range(3):
                s = 3 * u2 + i
                sc[pl.ds(SLOT * p + s, TROWS, stride=2 * SLOT), :] = o_sc[3 * p + i, rows, :].astype(F32)
                logs = jnp.where(lane == s, log_sc[3 * p + i, rows, :], logs)
        for part in range(3):
            rounded = logs.astype(BF).astype(F32)
            sc[pl.ds(SLOT * p + PAIRS + part, TROWS, stride=2 * SLOT), :] = rounded
            logs = logs - rounded
    slots[...] = sc[...].astype(BF).reshape(DEVS, SLOT, D)
    leave(slots, out_ref, sems)


def text_attention(length, text, kv, o, log):
    return pl.pallas_call(
        text_body,
        in_specs=[SMEM] + [ANY] * (2 * GROUP + 3),
        out_specs=ANY,
        out_shape=jax.ShapeDtypeStruct((DEVS, SLOT, D), BF),
        scratch_shapes=text_scratch(CHUNKS[1][1])
        + [
            pltpu.VMEM((HD, TXT, D), BF),
            pltpu.VMEM((HD, TXT, D), F32),
            pltpu.VMEM((DEVS * SLOT, D), F32),
            pltpu.VMEM((DEVS, SLOT, D), BF),
            pltpu.SemaphoreType.DMA((24,)),
        ],
        compiler_params=PARAMS,
        name="text_attention",
    )(length, *text, kv, o, log)


def leave(held, out_ref, sems):
    size = held.shape[0] // 4
    parts = [pl.ds(i * size, size) for i in range(4)]
    moves = copy_list([(held.at[x], out_ref.at[x]) for x in parts], sems)
    run(moves)
    wait(moves)


def combine_body(in_ref, out_ref, sc, res, slots, got, sems):
    leave(in_ref, got, sems)
    sc[...] = got[...].astype(F32).reshape(DEVS * SLOT, D)
    logs = sc[pl.ds(PAIRS, DEVS, stride=SLOT), :]
    for part in range(1, 3):
        logs = logs + sc[pl.ds(PAIRS + part, DEVS, stride=SLOT), :]
    logs = jnp.transpose(logs)[:SLOT]
    group = lax.broadcasted_iota(jnp.int32, (SLOT, DEVS), 1) % GROUP
    top = jnp.zeros((SLOT, DEVS), F32)
    for u in range(GROUP):
        best = jnp.max(jnp.where(group == u, logs, -jnp.inf), axis=1, keepdims=True)
        top = jnp.where(group == u, best, top)
    weights = jnp.exp2(logs - top)
    total = jnp.ones((SLOT, DEVS), F32)
    for u in range(GROUP):
        all_u = jnp.sum(jnp.where(group == u, weights, 0.0), axis=1, keepdims=True)
        total = jnp.where(group == u, all_u, total)
    weights = weights / total
    mine = lax.broadcasted_iota(jnp.int32, (8, DEVS), 1) % GROUP == lax.broadcasted_iota(jnp.int32, (8, DEVS), 0)
    res[...] = jnp.zeros_like(res)
    for u2 in range(GROUP):
        for i in range(3):
            s = 3 * u2 + i
            left = jnp.where(mine, jnp.broadcast_to(weights[s : s + 1], (8, DEVS)), 0.0)
            values = sc[pl.ds(s, DEVS, stride=SLOT), :]
            got = jnp.dot(left, values, preferred_element_type=F32, precision=lax.Precision.HIGHEST)
            for u in range(GROUP):
                res[u2, pl.ds(3 * u + i, 1), :] = got[u : u + 1]
    done = res[...].astype(BF)
    for b in range(BLK):
        slots[b] = done
    leave(slots, out_ref, sems)


def combine(received):
    return pl.pallas_call(
        combine_body,
        in_specs=[ANY],
        out_specs=ANY,
        out_shape=jax.ShapeDtypeStruct((BLK, GROUP, SLOT, D), BF),
        scratch_shapes=[
            pltpu.VMEM((DEVS * SLOT, D), F32),
            pltpu.VMEM((GROUP, SLOT, D), F32),
            pltpu.VMEM((BLK, GROUP, SLOT, D), BF),
            pltpu.VMEM((DEVS, SLOT, D), BF),
            pltpu.SemaphoreType.DMA((4,)),
        ],
        compiler_params=PARAMS,
        name="combine",
    )(received).reshape(DEVS, SLOT, D)


def video_body(first, heads, tiles, length, *refs):
    q_refs, text, refs = refs[:GROUP], refs[GROUP : 3 * GROUP], refs[3 * GROUP :]
    before, own, after, refs = refs[0], refs[1], refs[2], refs[3:]
    o_refs, refs = refs[:GROUP], refs[GROUP:]
    q_sc, k_sc, v_sc, t_sc, o_sc, side_sc, sems, text_sems, o_sems = refs

    def loads(h, a):
        sc = (k_sc, v_sc)[a]
        pairs = [(kv.at[:, a, h], sc.at[h, n]) for n, kv in enumerate((before, own, after))]
        return copy_list(pairs, sems.at[h, a])

    asked = pl.ds(first, heads)
    pairs = [(q_refs[d].at[0, asked], q_sc.at[:, rows_of(place(-d), ROWS)]) for d in range(GROUP)]
    shared = copy_list(pairs + text_loads(text, first, heads, None, t_sc), text_sems)
    run(loads(0, 0))
    run(shared)
    run(loads(0, 1))
    for h in range(1, heads):
        run(loads(h, 0))
        run(loads(h, 1))

    def stores(h):
        return [
            pltpu.make_async_copy(o_sc.at[h, rows_of(place(d), ROWS)], o_refs[d].at[h], o_sems.at[h, d])
            for d in range(GROUP)
        ]

    limit = (lax.axis_index("blk") + 1) * tiles.shape[0]
    for j in range(tiles.shape[0]):
        last = tiles[j, 0]
        for w in range(1, tiles.shape[1]):
            last = jnp.maximum(last, tiles[j, w])
        side_sc[j] = (last >= limit).astype(jnp.int32)
    live = text_bias(length[0])

    def step(h, i):
        f = pl.ds(side_sc[i * RB // TILE], 2)
        q = q_sc[h, i * RB : (i + 1) * RB, :]
        window = 2 * SLICE
        return weigh(
            q,
            lambda: k_sc[h, f].reshape(window, D),
            lambda: v_sc[h, f].reshape(window, D),
            lambda: t_sc[0, h],
            lambda: t_sc[1, h],
            live,
        )

    steps = SLICE // RB
    wait(loads(0, 0) + shared)

    def one(h, _):
        @pl.when(h > 0)
        def _():
            wait(loads(h, 0))

        rest = step(h, 0)
        wait(loads(h, 1))
        for i in range(steps):
            following = step(h, i + 1) if i + 1 < steps else None
            o, _ = rest()
            o_sc[h, i * RB : (i + 1) * RB, :] = o.astype(BF)
            rest = following
        run(stores(h))
        return 0

    lax.fori_loop(0, heads, one, 0)
    for h in range(heads):
        wait(stores(h))


def video_attention(first, heads, tiles, length, q, text, before, own, after):
    return pl.pallas_call(
        functools.partial(video_body, first, heads),
        in_specs=[SMEM, SMEM] + [ANY] * (3 * GROUP + 3),
        out_specs=[ANY] * GROUP,
        out_shape=[jax.ShapeDtypeStruct((heads, ROWS, D), BF)] * GROUP,
        scratch_shapes=[
            pltpu.VMEM((heads, SLICE, D), BF),
            pltpu.VMEM((heads, 3, GROUP, ROWS, D), BF),
            pltpu.VMEM((heads, 3, GROUP, ROWS, D), BF),
            pltpu.VMEM((2, heads, TXT, D), BF),
            pltpu.VMEM((heads, SLICE, D), BF),
            pltpu.SMEM((8,), jnp.int32),
            pltpu.SemaphoreType.DMA((heads, 2, 3)),
            pltpu.SemaphoreType.DMA((12,)),
            pltpu.SemaphoreType.DMA((heads, GROUP)),
        ],
        compiler_params=PARAMS,
        name="video_attention",
    )(tiles, length, *q, *text, before, own, after)


def rows_body(first, heads, *refs):
    pieces, refs = refs[:GROUP], refs[-4:]
    video_out, held, in_sems, out_sems = refs
    reads, writes = [], []
    for d in range(GROUP):
        for h in range(heads):
            n = len(reads)
            reads.append(pltpu.make_async_copy(pieces[d].at[h], held.at[n], in_sems.at[n]))
            there = video_out.at[:, column(place(-d) * HD + first + h)]
            writes.append(pltpu.make_async_copy(held.at[n], there, out_sems.at[n]))
    run(reads)
    for read, write in zip(reads, writes):
        read.wait()
        write.start()
    return writes


def first_body(first, heads, *refs):
    pieces, slots, video_out, text_out, held, sc, got, in_sems, out_sems, sems = refs[:GROUP], *refs[GROUP:]
    writes = rows_body(first, heads, *pieces, video_out, held, in_sems, out_sems)
    leave(slots, got, sems)
    sc[...] = got[...].astype(F32).reshape(DEVS * SLOT, D)
    for p in range(2):
        for u in range(GROUP):
            for i in range(3):
                rows = sc[pl.ds(SLOT * p + 3 * u + i, TROWS, stride=2 * SLOT), :]
                head = HD * u + 3 * p + i
                text_out[:, head * D : (head + 1) * D] = rows.astype(BF)
    wait(writes)


def later_body(first, heads, *refs):
    wait(rows_body(first, heads, *refs))


def first_rows(pieces, slots, first, heads):
    return pl.pallas_call(
        functools.partial(first_body, first, heads),
        in_specs=[ANY] * (GROUP + 1),
        out_specs=[ANY, VMEM],
        out_shape=[
            jax.ShapeDtypeStruct((ROWS, HEADS * D), BF),
            jax.ShapeDtypeStruct((TROWS, HEADS * D), BF),
        ],
        scratch_shapes=[
            pltpu.VMEM((GROUP * heads, ROWS, D), BF),
            pltpu.VMEM((DEVS * SLOT, D), F32),
            pltpu.VMEM((DEVS, SLOT, D), BF),
            pltpu.SemaphoreType.DMA((GROUP * heads,)),
            pltpu.SemaphoreType.DMA((GROUP * heads,)),
            pltpu.SemaphoreType.DMA((4,)),
        ],
        compiler_params=PARAMS,
        name="first_rows",
    )(*pieces, slots)


def later_rows(pieces, rows, first, heads):
    return pl.pallas_call(
        functools.partial(later_body, first, heads),
        in_specs=[ANY] * (GROUP + 1),
        out_specs=ANY,
        out_shape=jax.ShapeDtypeStruct((ROWS, HEADS * D), BF),
        scratch_shapes=[
            pltpu.VMEM((GROUP * heads, ROWS, D), BF),
            pltpu.SemaphoreType.DMA((GROUP * heads,)),
            pltpu.SemaphoreType.DMA((GROUP * heads,)),
        ],
        input_output_aliases={GROUP: 0},
        compiler_params=PARAMS,
        name="later_rows",
    )(*pieces, rows)


def local(video_q, video_k, video_v, text_q, text_k, text_v, window_tiles, text_len):
    video, words = (video_q, video_k, video_v), (text_q, text_k, text_v)
    (f0, n0), (f1, n1) = CHUNKS
    (kv0,) = pack(video, [((1, 2), f0, n0, ROWS, True)])
    text, kv1, q = pack(
        video + words,
        [
            ((3, 4, 5), 0, HD, HALF, False),
            ((1, 2), f1, n1, ROWS, True),
            ((0,), 0, HD, ROWS, False),
        ],
    )
    own, before, after = [], [], []
    for kv in (kv0, kv1):
        own.append(swap(kv, "uly"))
        before.append(beside(own[-1], 1))
        after.append(beside(own[-1], -1))
    mine = exchange(text[:GROUP])
    other = [text[GROUP]]
    for d in range(1, GROUP):
        other.append(lax.ppermute(mine[d], "blk", [(i, i ^ 1) for i in range(BLK)]))
    text = mine + other
    q = exchange(q)
    early = early_text(text_len, text, own[0])
    slots = text_attention(text_len, text, own[1], *early)
    slots = swap(slots, ("blk", "uly"))
    slots = combine(slots)
    slots = swap(slots, ("blk", "uly"))
    back = []
    for c, (first, heads) in enumerate(CHUNKS):
        o = video_attention(first, heads, window_tiles, text_len, q, text, before[c], own[c], after[c])
        back.append(exchange(o))
    rows, text_out = first_rows(back[0], slots, f0, n0)
    return later_rows(back[1], rows, f1, n1), text_out


def solution(mesh):
    in_specs = (
        P(("blk", "uly"), None),
        P(("blk", "uly"), None),
        P(("blk", "uly"), None),
        P("uly", None),
        P("uly", None),
        P("uly", None),
        P("blk", None),
        P(),
    )
    out_specs = (P(("blk", "uly"), None), P("uly", None))

    return jax.shard_map(local, mesh=mesh, in_specs=in_specs, out_specs=out_specs, check_vma=False)
```

```python
import functools
import math

import jax
import jax.numpy as jnp
from jax import lax
from jax.experimental import pallas as pl
from jax.experimental.pallas import tpu as pltpu
from jax.sharding import PartitionSpec as P


HEADS = 24
D = 128
TXT = 256
GROUP = 4
HD = HEADS // GROUP
ROWS = 288
SLICE = ROWS * GROUP
TILE = 384
TROWS = TXT // GROUP
HALF = TROWS // 2
BLK = 32
DEVS = GROUP * BLK
RB = 128
KEYS = 2 * SLICE + TXT
SCALE = math.log2(math.e) / math.sqrt(D)
CHUNKS = ((0, 4), (4, 2))
LIMIT = 67043328
BF = jnp.bfloat16
F32 = jnp.float32


ANY = pl.BlockSpec(memory_space=pl.ANY)
PARAMS = pltpu.CompilerParams(vmem_limit_bytes=LIMIT)
SMEM = pl.BlockSpec(memory_space=pltpu.SMEM)
VMEM = pl.BlockSpec(memory_space=pltpu.VMEM)


def place(distance):
    return (lax.axis_index("uly") + distance + GROUP) % GROUP


def half(which):
    return (lax.axis_index("blk") + which) % 2


def column(head):
    return pl.ds(pl.multiple_of(head * D, D), D)


def rows_of(position, count):
    return pl.ds(pl.multiple_of(position * count, 32), count)


def run(moves):
    for move in moves:
        move.start()


def wait(moves):
    for move in moves:
        move.wait()


def copy_list(pairs, sems):
    return [pltpu.make_async_copy(a, b, sems.at[i]) for i, (a, b) in enumerate(pairs)]


def pack(arrays, jobs):
    outs = []
    for numbers, _, heads, rows, together in jobs:
        shape = (len(numbers), heads, rows, D)
        if together:
            outs.append(jax.ShapeDtypeStruct((GROUP, *shape), BF))
        else:
            outs += [jax.ShapeDtypeStruct(shape, BF)] * (GROUP + (rows == HALF))

    def body(*refs):
        ins, rest = refs[: len(arrays)], refs[len(arrays) :]
        dst, held, in_sems, out_sems = rest[: len(outs)], rest[len(outs) : -2], rest[-2], rest[-1]
        reads, writes, n = [], [], 0
        for numbers, first, heads, rows, together in jobs:
            for d in range(GROUP + (rows == HALF)):
                which = slice(None) if rows == ROWS else rows_of(half(d // GROUP), rows)
                group = d if together else place(d % GROUP)
                here = held[n].at[d] if together else held[n]
                there = dst[n].at[d] if together else dst[n]
                pairs = [
                    (ins[k].at[which, column(group * HD + first + h)], here.at[i, h])
                    for i, k in enumerate(numbers)
                    for h in range(heads)
                ]
                base = sum(len(r) for r in reads)
                reads.append([pltpu.make_async_copy(x, y, in_sems.at[base + i]) for i, (x, y) in enumerate(pairs)])
                writes.append(pltpu.make_async_copy(here, there, out_sems.at[len(writes)]))
                n += not together
            n += together
        for read in reads:
            run(read)
        for read, write in zip(reads, writes):
            wait(read)
            write.start()
        wait(writes)

    got = pl.pallas_call(
        body,
        in_specs=[ANY] * len(arrays),
        out_specs=[ANY] * len(outs),
        out_shape=outs,
        scratch_shapes=[pltpu.VMEM(o.shape, BF) for o in outs]
        + [pltpu.SemaphoreType.DMA((160,)), pltpu.SemaphoreType.DMA((32,))],
        compiler_params=PARAMS,
    )(*arrays)
    result, n = [], 0
    for job in jobs:
        count = 1 if job[4] else GROUP + (job[3] == HALF)
        result.append(got[n] if job[4] else got[n : n + count])
        n += count
    return result


def around(block, distance):
    return lax.ppermute(block, "uly", [(i, (i + distance) % GROUP) for i in range(GROUP)])


def exchange(pieces):
    got = [pieces[0]]
    for d in range(1, GROUP):
        got.append(around(pieces[d], d))
    return got


def swap(array, axes):
    return lax.all_to_all(array, axes, 0, 0, tiled=True)


def beside(block, distance):
    return lax.ppermute(block, "blk", [(i, i + distance) for i in range(BLK) if 0 <= i + distance < BLK])


def text_bias(length):
    lane = lax.broadcasted_iota(jnp.int32, (1, TXT), 1)
    which = (lane // (TXT // 2) + half(0)) % 2
    source = (lax.axis_index("uly") + GROUP - lane % (TXT // 2) // HALF) % GROUP
    position = source * TROWS + which * HALF + lane % HALF
    return jnp.where(position < length, 0.0, -jnp.inf).astype(F32)


def weigh(q, keys, values, masked):
    s = lax.dot_general(q, keys(), (((1,), (1,)), ((), ())), preferred_element_type=F32)

    def finish():
        parts, at = [], 0
        for start, bias in masked:
            if start > at:
                parts.append(s[:, at:start])
            parts.append(s[:, start : start + TXT] + bias)
            at = start + TXT
        if at < s.shape[1]:
            parts.append(s[:, at:])
        whole = jnp.concatenate(parts, axis=1)
        top = jnp.max(whole, axis=1, keepdims=True) * SCALE
        p = jnp.exp2(whole * SCALE - top)
        total = jnp.sum(p, axis=1, keepdims=True)
        o = jnp.dot(p.astype(BF), values(), preferred_element_type=F32)
        return o / total, top + jnp.log2(total)

    return finish


SLOT = 16
PAIRS = 12


def text_body(length, *refs):
    text, kv, refs = refs[: 2 * GROUP], refs[2 * GROUP :][: len(CHUNKS)], refs[2 * GROUP + len(CHUNKS) :]
    out_ref, q_sc, kv_sc, o_sc, log_sc, sc, slots, sems = refs
    pairs = []
    for n, piece in enumerate(text):
        rows = rows_of(2 * place(-(n % GROUP)) + half(n // GROUP), HALF)
        pairs.append((piece.at[0], q_sc.at[:, rows]))
        pairs.append((piece.at[pl.ds(1, 2)], kv_sc.at[:, :, pl.ds(SLICE + n * HALF, HALF)]))
    for c, (first, heads) in enumerate(CHUNKS):
        for g in range(GROUP):
            pairs.append((kv[c].at[g], kv_sc.at[:, pl.ds(first, heads), pl.ds(g * ROWS, ROWS)]))
    moves = copy_list(pairs, sems)
    run(moves)
    sc[...] = jnp.zeros_like(sc)
    bias = jnp.where(lax.axis_index("blk") == 0, text_bias(length[0]), -jnp.inf)
    wait(moves)
    steps = [(h, i) for h in range(HD) for i in range(TXT // RB)]

    def begin(h, i):
        q = q_sc[h, i * RB : (i + 1) * RB]
        return weigh(q, lambda: kv_sc[0, h], lambda: kv_sc[1, h], [(SLICE, bias)])

    rest = begin(*steps[0])
    for n, (h, i) in enumerate(steps):
        following = begin(*steps[n + 1]) if n + 1 < len(steps) else None
        o, log = rest()
        o_sc[h, i * RB : (i + 1) * RB] = o
        log_sc[h, i * RB : (i + 1) * RB] = jnp.broadcast_to(log, (RB, D))
        rest = following
    lane = lax.broadcasted_iota(jnp.int32, (TROWS, D), 1)
    for p in range(2):
        logs = jnp.zeros((TROWS, D), F32)
        for u2 in range(GROUP):
            rows = pl.ds(u2 * TROWS, TROWS)
            for i in range(3):
                s = 3 * u2 + i
                sc[pl.ds(SLOT * p + s, TROWS, stride=2 * SLOT), :] = o_sc[3 * p + i, rows, :]
                logs = jnp.where(lane == s, log_sc[3 * p + i, rows, :], logs)
        for part in range(3):
            rounded = logs.astype(BF).astype(F32)
            sc[pl.ds(SLOT * p + PAIRS + part, TROWS, stride=2 * SLOT), :] = rounded
            logs = logs - rounded
    slots[...] = sc[...].astype(BF).reshape(DEVS, SLOT, D)
    leave(slots, out_ref, sems)


def leave(held, out_ref, sems):
    size = held.shape[0] // 4
    parts = [pl.ds(i * size, size) for i in range(4)]
    moves = copy_list([(held.at[x], out_ref.at[x]) for x in parts], sems)
    run(moves)
    wait(moves)


def text_attention(length, text, kv):
    return pl.pallas_call(
        text_body,
        in_specs=[SMEM] + [ANY] * (2 * GROUP + len(CHUNKS)),
        out_specs=ANY,
        out_shape=jax.ShapeDtypeStruct((DEVS, SLOT, D), BF),
        scratch_shapes=[
            pltpu.VMEM((HD, TXT, D), BF),
            pltpu.VMEM((2, HD, SLICE + TXT, D), BF),
            pltpu.VMEM((HD, TXT, D), F32),
            pltpu.VMEM((HD, TXT, D), F32),
            pltpu.VMEM((DEVS * SLOT, D), F32),
            pltpu.VMEM((DEVS, SLOT, D), BF),
            pltpu.SemaphoreType.DMA((32,)),
        ],
        compiler_params=PARAMS,
        name="text_attention",
    )(length, *text, *kv)


def combine_body(in_ref, out_ref, sc, res, slots, got, sems):
    leave(in_ref, got, sems)
    sc[...] = got[...].astype(F32).reshape(DEVS * SLOT, D)
    logs = sc[pl.ds(PAIRS, DEVS, stride=SLOT), :]
    for part in range(1, 3):
        logs = logs + sc[pl.ds(PAIRS + part, DEVS, stride=SLOT), :]
    logs = jnp.transpose(logs)[:SLOT]
    group = lax.broadcasted_iota(jnp.int32, (SLOT, DEVS), 1) % GROUP
    top = jnp.zeros((SLOT, DEVS), F32)
    for u in range(GROUP):
        best = jnp.max(jnp.where(group == u, logs, -jnp.inf), axis=1, keepdims=True)
        top = jnp.where(group == u, best, top)
    weights = jnp.exp2(logs - top)
    total = jnp.ones((SLOT, DEVS), F32)
    for u in range(GROUP):
        all_u = jnp.sum(jnp.where(group == u, weights, 0.0), axis=1, keepdims=True)
        total = jnp.where(group == u, all_u, total)
    weights = weights / total
    mine = lax.broadcasted_iota(jnp.int32, (8, DEVS), 1) % GROUP == lax.broadcasted_iota(jnp.int32, (8, DEVS), 0)
    res[...] = jnp.zeros_like(res)
    for u2 in range(GROUP):
        for i in range(3):
            s = 3 * u2 + i
            left = jnp.where(mine, jnp.broadcast_to(weights[s : s + 1], (8, DEVS)), 0.0)
            values = sc[pl.ds(s, DEVS, stride=SLOT), :]
            got = jnp.dot(left, values, preferred_element_type=F32, precision=lax.Precision.HIGHEST)
            for u in range(GROUP):
                res[u2, pl.ds(3 * u + i, 1), :] = got[u : u + 1]
    done = res[...].astype(BF)
    for b in range(BLK):
        slots[b] = done
    leave(slots, out_ref, sems)


def combine(received):
    return pl.pallas_call(
        combine_body,
        in_specs=[ANY],
        out_specs=ANY,
        out_shape=jax.ShapeDtypeStruct((BLK, GROUP, SLOT, D), BF),
        scratch_shapes=[
            pltpu.VMEM((DEVS * SLOT, D), F32),
            pltpu.VMEM((GROUP, SLOT, D), F32),
            pltpu.VMEM((BLK, GROUP, SLOT, D), BF),
            pltpu.VMEM((DEVS, SLOT, D), BF),
            pltpu.SemaphoreType.DMA((4,)),
        ],
        compiler_params=PARAMS,
        name="combine",
    )(received).reshape(DEVS, SLOT, D)


def video_body(first, heads, tiles, length, *refs):
    q_refs, text, refs = refs[:GROUP], refs[GROUP : 3 * GROUP], refs[3 * GROUP :]
    before, own, after, refs = refs[0], refs[1], refs[2], refs[3:]
    o_refs, refs = refs[:GROUP], refs[GROUP:]
    q_sc, k_sc, v_sc, o_sc, side_sc, sems, shared_sems, o_sems = refs

    def loads(start, count, a):
        some, pairs = pl.ds(start, count), []
        for base, kv in ((0, before), (SLICE, own), (KEYS, after)):
            for g in range(GROUP):
                pairs.append((kv.at[g, a, some], (k_sc, v_sc)[a].at[some, pl.ds(base + g * ROWS, ROWS)]))
        return copy_list(pairs, sems.at[min(start, 1), a])

    others = loads(1, heads - 1, 0) + loads(1, heads - 1, 1)
    asked = pl.ds(first, heads)
    shared = [[(q_refs[d].at[0, asked], q_sc.at[:, rows_of(place(-d), ROWS)]) for d in range(GROUP)], []]
    for a, sc in ((0, k_sc), (1, v_sc)):
        for n, piece in enumerate(text):
            shared[a].append((piece.at[1 + a, asked], sc.at[:, pl.ds(2 * SLICE + n * HALF, HALF)]))
    shared = [copy_list(pairs, shared_sems.at[a]) for a, pairs in enumerate(shared)]
    run(loads(0, 1, 0))
    run(shared[0])
    run(loads(0, 1, 1))
    run(shared[1])
    run(others)

    def stores(h):
        return [
            pltpu.make_async_copy(o_sc.at[h, rows_of(place(d), ROWS)], o_refs[d].at[h], o_sems.at[h, d])
            for d in range(GROUP)
        ]

    limit = (lax.axis_index("blk") + 1) * tiles.shape[0]
    for j in range(tiles.shape[0]):
        last = tiles[j, 0]
        for w in range(1, tiles.shape[1]):
            last = jnp.maximum(last, tiles[j, w])
        side_sc[j] = (last >= limit).astype(jnp.int32)
    live = text_bias(length[0])

    def step(h, i):
        f = side_sc[i * RB // TILE]
        window = pl.ds(pl.multiple_of(f * SLICE, RB), KEYS)
        masked = [(SLICE, jnp.where(f == 1, live, 0.0)), (2 * SLICE, jnp.where(f == 1, 0.0, live))]
        q = q_sc[h, i * RB : (i + 1) * RB, :]
        return weigh(q, lambda: k_sc[h, window], lambda: v_sc[h, window], masked)

    steps = SLICE // RB
    wait(loads(0, 1, 0) + shared[0])

    def one(h, _):
        @pl.when(h == 1)
        def _():
            wait(others)

        rest = step(h, 0)

        @pl.when(h == 0)
        def _():
            wait(loads(0, 1, 1) + shared[1])

        for i in range(steps):
            following = step(h, i + 1) if i + 1 < steps else None
            o, _ = rest()
            o_sc[h, i * RB : (i + 1) * RB, :] = o.astype(BF)
            rest = following
        run(stores(h))
        return 0

    lax.fori_loop(0, heads, one, 0)
    for h in range(heads):
        wait(stores(h))


def video_attention(first, heads, tiles, length, q, text, before, own, after):
    return pl.pallas_call(
        functools.partial(video_body, first, heads),
        in_specs=[SMEM, SMEM] + [ANY] * (3 * GROUP + 3),
        out_specs=[ANY] * GROUP,
        out_shape=[jax.ShapeDtypeStruct((heads, ROWS, D), BF)] * GROUP,
        scratch_shapes=[
            pltpu.VMEM((heads, SLICE, D), BF),
            pltpu.VMEM((heads, KEYS + SLICE, D), BF),
            pltpu.VMEM((heads, KEYS + SLICE, D), BF),
            pltpu.VMEM((heads, SLICE, D), BF),
            pltpu.SMEM((8,), jnp.int32),
            pltpu.SemaphoreType.DMA((2, 2, 12)),
            pltpu.SemaphoreType.DMA((2, 12)),
            pltpu.SemaphoreType.DMA((heads, GROUP)),
        ],
        compiler_params=PARAMS,
        name="video_attention",
    )(tiles, length, *q, *text, before, own, after)


def rows_body(first, heads, *refs):
    pieces, refs = refs[:GROUP], refs[-4:]
    video_out, held, in_sems, out_sems = refs
    reads, writes = [], []
    for d in range(GROUP):
        for h in range(heads):
            n = len(reads)
            reads.append(pltpu.make_async_copy(pieces[d].at[h], held.at[n], in_sems.at[n]))
            there = video_out.at[:, column(place(-d) * HD + first + h)]
            writes.append(pltpu.make_async_copy(held.at[n], there, out_sems.at[n]))
    run(reads)
    for read, write in zip(reads, writes):
        read.wait()
        write.start()
    return writes


def first_body(first, heads, *refs):
    pieces, slots, video_out, text_out, held, sc, got, in_sems, out_sems, sems = refs[:GROUP], *refs[GROUP:]
    writes = rows_body(first, heads, *pieces, video_out, held, in_sems, out_sems)
    leave(slots, got, sems)
    sc[...] = got[...].astype(F32).reshape(DEVS * SLOT, D)
    for p in range(2):
        for u in range(GROUP):
            for i in range(3):
                rows = sc[pl.ds(SLOT * p + 3 * u + i, TROWS, stride=2 * SLOT), :]
                head = HD * u + 3 * p + i
                text_out[:, head * D : (head + 1) * D] = rows.astype(BF)
    wait(writes)


def later_body(first, heads, *refs):
    wait(rows_body(first, heads, *refs))


def first_rows(pieces, slots, first, heads):
    return pl.pallas_call(
        functools.partial(first_body, first, heads),
        in_specs=[ANY] * (GROUP + 1),
        out_specs=[ANY, VMEM],
        out_shape=[
            jax.ShapeDtypeStruct((ROWS, HEADS * D), BF),
            jax.ShapeDtypeStruct((TROWS, HEADS * D), BF),
        ],
        scratch_shapes=[
            pltpu.VMEM((GROUP * heads, ROWS, D), BF),
            pltpu.VMEM((DEVS * SLOT, D), F32),
            pltpu.VMEM((DEVS, SLOT, D), BF),
            pltpu.SemaphoreType.DMA((GROUP * heads,)),
            pltpu.SemaphoreType.DMA((GROUP * heads,)),
            pltpu.SemaphoreType.DMA((4,)),
        ],
        compiler_params=PARAMS,
        name="first_rows",
    )(*pieces, slots)


def later_rows(pieces, rows, first, heads):
    return pl.pallas_call(
        functools.partial(later_body, first, heads),
        in_specs=[ANY] * (GROUP + 1),
        out_specs=ANY,
        out_shape=jax.ShapeDtypeStruct((ROWS, HEADS * D), BF),
        scratch_shapes=[
            pltpu.VMEM((GROUP * heads, ROWS, D), BF),
            pltpu.SemaphoreType.DMA((GROUP * heads,)),
            pltpu.SemaphoreType.DMA((GROUP * heads,)),
        ],
        input_output_aliases={GROUP: 0},
        compiler_params=PARAMS,
        name="later_rows",
    )(*pieces, rows)


def local(video_q, video_k, video_v, text_q, text_k, text_v, window_tiles, text_len):
    video, words = (video_q, video_k, video_v), (text_q, text_k, text_v)
    (f0, n0), (f1, n1) = CHUNKS
    (kv0,) = pack(video, [((1, 2), f0, n0, ROWS, True)])
    text, kv1, q = pack(
        video + words,
        [
            ((3, 4, 5), 0, HD, HALF, False),
            ((1, 2), f1, n1, ROWS, True),
            ((0,), 0, HD, ROWS, False),
        ],
    )
    own, before, after = [], [], []
    for kv in (kv0, kv1):
        own.append(swap(kv, "uly"))
        before.append(beside(own[-1], 1))
        after.append(beside(own[-1], -1))
    mine = exchange(text[:GROUP])
    other = [text[GROUP]]
    for d in range(1, GROUP):
        other.append(lax.ppermute(mine[d], "blk", [(i, i ^ 1) for i in range(BLK)]))
    text = mine + other
    q = exchange(q)
    slots = text_attention(text_len, text, own)
    slots = swap(slots, ("blk", "uly"))
    slots = combine(slots)
    slots = swap(slots, ("blk", "uly"))
    back = []
    for c, (first, heads) in enumerate(CHUNKS):
        o = video_attention(first, heads, window_tiles, text_len, q, text, before[c], own[c], after[c])
        back.append(exchange(o))
    rows, text_out = first_rows(back[0], slots, f0, n0)
    return later_rows(back[1], rows, f1, n1), text_out


def solution(mesh):
    in_specs = (
        P(("blk", "uly"), None),
        P(("blk", "uly"), None),
        P(("blk", "uly"), None),
        P("uly", None),
        P("uly", None),
        P("uly", None),
        P("blk", None),
        P(),
    )
    out_specs = (P(("blk", "uly"), None), P("uly", None))

    return jax.shard_map(local, mesh=mesh, in_specs=in_specs, out_specs=out_specs, check_vma=False)
```

```python
import functools
import math

import jax
import jax.numpy as jnp
from jax import lax
from jax.experimental import pallas as pl
from jax.experimental.pallas import tpu as pltpu
from jax.sharding import PartitionSpec as P


HEADS = 24
D = 128
TXT = 256
GROUP = 4
HD = HEADS // GROUP
ROWS = 288
SLICE = ROWS * GROUP
TILE = 384
TROWS = TXT // GROUP
HALF = TROWS // 2
BLK = 32
DEVS = GROUP * BLK
RB = 128
KEYS = 2 * SLICE + TXT
SCALE = math.log2(math.e) / math.sqrt(D)
CHUNKS = ((0, 4), (4, 2))
LIMIT = 67043328
BF = jnp.bfloat16
F32 = jnp.float32


ANY = pl.BlockSpec(memory_space=pl.ANY)
PARAMS = pltpu.CompilerParams(vmem_limit_bytes=LIMIT)
SMEM = pl.BlockSpec(memory_space=pltpu.SMEM)
VMEM = pl.BlockSpec(memory_space=pltpu.VMEM)


def place(distance):
    return (lax.axis_index("uly") + distance + GROUP) % GROUP


def half(which):
    return (lax.axis_index("blk") + which) % 2


def column(head):
    return pl.ds(pl.multiple_of(head * D, D), D)


def rows_of(position, count):
    return pl.ds(pl.multiple_of(position * count, 32), count)


def run(moves):
    for move in moves:
        move.start()


def wait(moves):
    for move in moves:
        move.wait()


def copy_list(pairs, sems):
    return [pltpu.make_async_copy(a, b, sems.at[i]) for i, (a, b) in enumerate(pairs)]


def pack(arrays, jobs):
    outs = []
    for numbers, _, heads, rows, together in jobs:
        shape = (len(numbers), heads, rows, D)
        if together:
            outs.append(jax.ShapeDtypeStruct((GROUP, *shape), BF))
        else:
            outs += [jax.ShapeDtypeStruct(shape, BF)] * (GROUP + (rows == HALF))

    def body(*refs):
        ins, rest = refs[: len(arrays)], refs[len(arrays) :]
        dst, held, in_sems, out_sems = rest[: len(outs)], rest[len(outs) : -2], rest[-2], rest[-1]
        reads, writes, n = [], [], 0
        for numbers, first, heads, rows, together in jobs:
            for d in range(GROUP + (rows == HALF)):
                which = slice(None) if rows == ROWS else rows_of(half(d // GROUP), rows)
                group = d if together else place(d % GROUP)
                here = held[n].at[d] if together else held[n]
                there = dst[n].at[d] if together else dst[n]
                pairs = [
                    (ins[k].at[which, column(group * HD + first + h)], here.at[i, h])
                    for i, k in enumerate(numbers)
                    for h in range(heads)
                ]
                base = sum(len(r) for r in reads)
                reads.append([pltpu.make_async_copy(x, y, in_sems.at[base + i]) for i, (x, y) in enumerate(pairs)])
                writes.append(pltpu.make_async_copy(here, there, out_sems.at[len(writes)]))
                n += not together
            n += together
        for read in reads:
            run(read)
        for read, write in zip(reads, writes):
            wait(read)
            write.start()
        wait(writes)

    got = pl.pallas_call(
        body,
        in_specs=[ANY] * len(arrays),
        out_specs=[ANY] * len(outs),
        out_shape=outs,
        scratch_shapes=[pltpu.VMEM(o.shape, BF) for o in outs]
        + [pltpu.SemaphoreType.DMA((160,)), pltpu.SemaphoreType.DMA((32,))],
        compiler_params=PARAMS,
    )(*arrays)
    result, n = [], 0
    for job in jobs:
        count = 1 if job[4] else GROUP + (job[3] == HALF)
        result.append(got[n] if job[4] else got[n : n + count])
        n += count
    return result


def around(block, distance):
    return lax.ppermute(block, "uly", [(i, (i + distance) % GROUP) for i in range(GROUP)])


def exchange(pieces):
    got = [pieces[0]]
    for d in range(1, GROUP):
        got.append(around(pieces[d], d))
    return got


def swap(array, axes):
    return lax.all_to_all(array, axes, 0, 0, tiled=True)


def beside(block, distance):
    return lax.ppermute(block, "blk", [(i, i + distance) for i in range(BLK) if 0 <= i + distance < BLK])


def text_bias(length):
    lane = lax.broadcasted_iota(jnp.int32, (1, TXT), 1)
    which = (lane // (TXT // 2) + half(0)) % 2
    source = (lax.axis_index("uly") + GROUP - lane % (TXT // 2) // HALF) % GROUP
    position = source * TROWS + which * HALF + lane % HALF
    return jnp.where(position < length, 0.0, -jnp.inf).astype(F32)


def weigh(q, keys, values, masked):
    s = lax.dot_general(q, keys(), (((1,), (1,)), ((), ())), preferred_element_type=F32)

    def finish():
        parts, at = [], 0
        for start, bias in masked:
            if start > at:
                parts.append(s[:, at:start])
            parts.append(s[:, start : start + TXT] + bias)
            at = start + TXT
        if at < s.shape[1]:
            parts.append(s[:, at:])
        whole = jnp.concatenate(parts, axis=1)
        top = jnp.max(whole, axis=1, keepdims=True) * SCALE
        p = jnp.exp2(whole * SCALE - top)
        total = jnp.sum(p, axis=1, keepdims=True)
        o = jnp.dot(p.astype(BF), values(), preferred_element_type=F32)
        return o / total, top + jnp.log2(total)

    return finish


SLOT = 16
PAIRS = 12


def text_body(length, *refs):
    text, kv, refs = refs[: 2 * GROUP], refs[2 * GROUP :][: len(CHUNKS)], refs[2 * GROUP + len(CHUNKS) :]
    out_ref, q_sc, kv_sc, o_sc, log_sc, sc, slots, sems = refs
    pairs, moves = [], []
    for n, piece in enumerate(text):
        rows = rows_of(2 * place(-(n % GROUP)) + half(n // GROUP), HALF)
        pairs.append((piece.at[0], q_sc.at[:, rows]))
        pairs.append((piece.at[pl.ds(1, 2)], kv_sc.at[:, :, pl.ds(SLICE + n * HALF, HALF)]))
    for c, (first, heads) in enumerate(CHUNKS):
        for g in range(GROUP):
            pairs.append((kv[c].at[g], kv_sc.at[:, pl.ds(first, heads), pl.ds(g * ROWS, ROWS)]))
        moves.append(copy_list(pairs, sems.at[c]))
        run(moves[-1])
        pairs = []
    sc[...] = jnp.zeros_like(sc)
    bias = jnp.where(lax.axis_index("blk") == 0, text_bias(length[0]), -jnp.inf)
    wait(moves[0])
    steps = [(h, i) for h in range(HD) for i in range(TXT // RB)]

    def begin(h, i):
        if (h, i) == (CHUNKS[1][0], 0):
            wait(moves[1])
        q = q_sc[h, i * RB : (i + 1) * RB]
        return weigh(q, lambda: kv_sc[0, h], lambda: kv_sc[1, h], [(SLICE, bias)])

    rest = begin(*steps[0])
    for n, (h, i) in enumerate(steps):
        following = begin(*steps[n + 1]) if n + 1 < len(steps) else None
        o, log = rest()
        o_sc[h, i * RB : (i + 1) * RB] = o
        log_sc[h, i * RB : (i + 1) * RB] = jnp.broadcast_to(log, (RB, D))
        rest = following
    lane = lax.broadcasted_iota(jnp.int32, (TROWS, D), 1)
    for p in range(2):
        logs = jnp.zeros((TROWS, D), F32)
        for u2 in range(GROUP):
            rows = pl.ds(u2 * TROWS, TROWS)
            for i in range(3):
                s = 3 * u2 + i
                sc[pl.ds(SLOT * p + s, TROWS, stride=2 * SLOT), :] = o_sc[3 * p + i, rows, :]
                logs = jnp.where(lane == s, log_sc[3 * p + i, rows, :], logs)
        for part in range(3):
            rounded = logs.astype(BF).astype(F32)
            sc[pl.ds(SLOT * p + PAIRS + part, TROWS, stride=2 * SLOT), :] = rounded
            logs = logs - rounded
    slots[...] = sc[...].astype(BF).reshape(DEVS, SLOT, D)
    leave(slots, out_ref, sems.at[0])


def leave(held, out_ref, sems):
    size = held.shape[0] // 4
    parts = [pl.ds(i * size, size) for i in range(4)]
    moves = copy_list([(held.at[x], out_ref.at[x]) for x in parts], sems)
    run(moves)
    wait(moves)


def text_attention(length, text, kv):
    return pl.pallas_call(
        text_body,
        in_specs=[SMEM] + [ANY] * (2 * GROUP + len(CHUNKS)),
        out_specs=ANY,
        out_shape=jax.ShapeDtypeStruct((DEVS, SLOT, D), BF),
        scratch_shapes=[
            pltpu.VMEM((HD, TXT, D), BF),
            pltpu.VMEM((2, HD, SLICE + TXT, D), BF),
            pltpu.VMEM((HD, TXT, D), F32),
            pltpu.VMEM((HD, TXT, D), F32),
            pltpu.VMEM((DEVS * SLOT, D), F32),
            pltpu.VMEM((DEVS, SLOT, D), BF),
            pltpu.SemaphoreType.DMA((2, 24)),
        ],
        compiler_params=PARAMS,
        name="text_attention",
    )(length, *text, *kv)


def combine_body(in_ref, out_ref, sc, res, slots, got, sems):
    leave(in_ref, got, sems)
    sc[...] = got[...].astype(F32).reshape(DEVS * SLOT, D)
    logs = sc[pl.ds(PAIRS, DEVS, stride=SLOT), :]
    for part in range(1, 3):
        logs = logs + sc[pl.ds(PAIRS + part, DEVS, stride=SLOT), :]
    logs = jnp.transpose(logs)[:SLOT]
    group = lax.broadcasted_iota(jnp.int32, (SLOT, DEVS), 1) % GROUP
    top = jnp.zeros((SLOT, DEVS), F32)
    for u in range(GROUP):
        best = jnp.max(jnp.where(group == u, logs, -jnp.inf), axis=1, keepdims=True)
        top = jnp.where(group == u, best, top)
    weights = jnp.exp2(logs - top)
    total = jnp.ones((SLOT, DEVS), F32)
    for u in range(GROUP):
        all_u = jnp.sum(jnp.where(group == u, weights, 0.0), axis=1, keepdims=True)
        total = jnp.where(group == u, all_u, total)
    weights = weights / total
    mine = lax.broadcasted_iota(jnp.int32, (8, DEVS), 1) % GROUP == lax.broadcasted_iota(jnp.int32, (8, DEVS), 0)
    res[...] = jnp.zeros_like(res)
    for u2 in range(GROUP):
        for i in range(3):
            s = 3 * u2 + i
            left = jnp.where(mine, jnp.broadcast_to(weights[s : s + 1], (8, DEVS)), 0.0)
            values = sc[pl.ds(s, DEVS, stride=SLOT), :]
            got = jnp.dot(left, values, preferred_element_type=F32, precision=lax.Precision.HIGHEST)
            for u in range(GROUP):
                res[u2, pl.ds(3 * u + i, 1), :] = got[u : u + 1]
    done = res[...].astype(BF)
    for b in range(BLK):
        slots[b] = done
    leave(slots, out_ref, sems)


def combine(received):
    return pl.pallas_call(
        combine_body,
        in_specs=[ANY],
        out_specs=ANY,
        out_shape=jax.ShapeDtypeStruct((BLK, GROUP, SLOT, D), BF),
        scratch_shapes=[
            pltpu.VMEM((DEVS * SLOT, D), F32),
            pltpu.VMEM((GROUP, SLOT, D), F32),
            pltpu.VMEM((BLK, GROUP, SLOT, D), BF),
            pltpu.VMEM((DEVS, SLOT, D), BF),
            pltpu.SemaphoreType.DMA((4,)),
        ],
        compiler_params=PARAMS,
        name="combine",
    )(received).reshape(DEVS, SLOT, D)


def video_body(first, heads, tiles, length, *refs):
    q_refs, text, refs = refs[:GROUP], refs[GROUP : 3 * GROUP], refs[3 * GROUP :]
    before, own, after, refs = refs[0], refs[1], refs[2], refs[3:]
    o_refs, refs = refs[:GROUP], refs[GROUP:]
    q_sc, k_sc, v_sc, o_sc, side_sc, sems, shared_sems, o_sems = refs

    def loads(start, count, a):
        some, pairs = pl.ds(start, count), []
        for base, kv in ((0, before), (SLICE, own), (KEYS, after)):
            for g in range(GROUP):
                pairs.append((kv.at[g, a, some], (k_sc, v_sc)[a].at[some, pl.ds(base + g * ROWS, ROWS)]))
        return copy_list(pairs, sems.at[min(start, 1), a])

    others = loads(1, heads - 1, 0) + loads(1, heads - 1, 1)
    asked = pl.ds(first, heads)
    shared = [[(q_refs[d].at[0, asked], q_sc.at[:, rows_of(place(-d), ROWS)]) for d in range(GROUP)], []]
    for a, sc in ((0, k_sc), (1, v_sc)):
        for n, piece in enumerate(text):
            shared[a].append((piece.at[1 + a, asked], sc.at[:, pl.ds(2 * SLICE + n * HALF, HALF)]))
    shared = [copy_list(pairs, shared_sems.at[a]) for a, pairs in enumerate(shared)]
    run(loads(0, 1, 0))
    run(shared[0])
    run(loads(0, 1, 1))
    run(shared[1])
    run(others)

    def stores(h):
        return [
            pltpu.make_async_copy(o_sc.at[h, rows_of(place(d), ROWS)], o_refs[d].at[h], o_sems.at[h, d])
            for d in range(GROUP)
        ]

    limit = (lax.axis_index("blk") + 1) * tiles.shape[0]
    for j in range(tiles.shape[0]):
        last = tiles[j, 0]
        for w in range(1, tiles.shape[1]):
            last = jnp.maximum(last, tiles[j, w])
        side_sc[j] = (last >= limit).astype(jnp.int32)
    live = text_bias(length[0])

    def step(h, i):
        f = side_sc[i * RB // TILE]
        window = pl.ds(pl.multiple_of(f * SLICE, RB), KEYS)
        masked = [(SLICE, jnp.where(f == 1, live, 0.0)), (2 * SLICE, jnp.where(f == 1, 0.0, live))]
        q = q_sc[h, i * RB : (i + 1) * RB, :]
        return weigh(q, lambda: k_sc[h, window], lambda: v_sc[h, window], masked)

    steps = SLICE // RB
    wait(loads(0, 1, 0) + shared[0])

    def one(h, _):
        @pl.when(h == 1)
        def _():
            wait(others)

        rest = step(h, 0)

        @pl.when(h == 0)
        def _():
            wait(loads(0, 1, 1) + shared[1])

        for i in range(steps):
            following = step(h, i + 1) if i + 1 < steps else None
            o, _ = rest()
            o_sc[h, i * RB : (i + 1) * RB, :] = o.astype(BF)
            rest = following
        run(stores(h))
        return 0

    lax.fori_loop(0, heads, one, 0)
    for h in range(heads):
        wait(stores(h))


def video_attention(first, heads, tiles, length, q, text, before, own, after):
    return pl.pallas_call(
        functools.partial(video_body, first, heads),
        in_specs=[SMEM, SMEM] + [ANY] * (3 * GROUP + 3),
        out_specs=[ANY] * GROUP,
        out_shape=[jax.ShapeDtypeStruct((heads, ROWS, D), BF)] * GROUP,
        scratch_shapes=[
            pltpu.VMEM((heads, SLICE, D), BF),
            pltpu.VMEM((heads, KEYS + SLICE, D), BF),
            pltpu.VMEM((heads, KEYS + SLICE, D), BF),
            pltpu.VMEM((heads, SLICE, D), BF),
            pltpu.SMEM((8,), jnp.int32),
            pltpu.SemaphoreType.DMA((2, 2, 12)),
            pltpu.SemaphoreType.DMA((2, 12)),
            pltpu.SemaphoreType.DMA((heads, GROUP)),
        ],
        compiler_params=PARAMS,
        name="video_attention",
    )(tiles, length, *q, *text, before, own, after)


def rows_body(first, heads, *refs):
    pieces, refs = refs[:GROUP], refs[-4:]
    video_out, held, in_sems, out_sems = refs
    reads, writes = [], []
    for d in range(GROUP):
        for h in range(heads):
            n = len(reads)
            reads.append(pltpu.make_async_copy(pieces[d].at[h], held.at[n], in_sems.at[n]))
            there = video_out.at[:, column(place(-d) * HD + first + h)]
            writes.append(pltpu.make_async_copy(held.at[n], there, out_sems.at[n]))
    run(reads)
    for read, write in zip(reads, writes):
        read.wait()
        write.start()
    return writes


def first_body(first, heads, *refs):
    pieces, slots, video_out, text_out, held, sc, got, in_sems, out_sems, sems = refs[:GROUP], *refs[GROUP:]
    fetch = pltpu.make_async_copy(slots, got, sems.at[0])
    fetch.start()
    writes = rows_body(first, heads, *pieces, video_out, held, in_sems, out_sems)
    fetch.wait()
    sc[...] = got[...].astype(F32).reshape(DEVS * SLOT, D)
    for p in range(2):
        for u in range(GROUP):
            for i in range(3):
                rows = sc[pl.ds(SLOT * p + 3 * u + i, TROWS, stride=2 * SLOT), :]
                head = HD * u + 3 * p + i
                text_out[:, head * D : (head + 1) * D] = rows.astype(BF)
    wait(writes)


def later_body(first, heads, *refs):
    wait(rows_body(first, heads, *refs))


def first_rows(pieces, slots, first, heads):
    return pl.pallas_call(
        functools.partial(first_body, first, heads),
        in_specs=[ANY] * (GROUP + 1),
        out_specs=[ANY, VMEM],
        out_shape=[
            jax.ShapeDtypeStruct((ROWS, HEADS * D), BF),
            jax.ShapeDtypeStruct((TROWS, HEADS * D), BF),
        ],
        scratch_shapes=[
            pltpu.VMEM((GROUP * heads, ROWS, D), BF),
            pltpu.VMEM((DEVS * SLOT, D), F32),
            pltpu.VMEM((DEVS, SLOT, D), BF),
            pltpu.SemaphoreType.DMA((GROUP * heads,)),
            pltpu.SemaphoreType.DMA((GROUP * heads,)),
            pltpu.SemaphoreType.DMA((4,)),
        ],
        compiler_params=PARAMS,
        name="first_rows",
    )(*pieces, slots)


def later_rows(pieces, rows, first, heads):
    return pl.pallas_call(
        functools.partial(later_body, first, heads),
        in_specs=[ANY] * (GROUP + 1),
        out_specs=ANY,
        out_shape=jax.ShapeDtypeStruct((ROWS, HEADS * D), BF),
        scratch_shapes=[
            pltpu.VMEM((GROUP * heads, ROWS, D), BF),
            pltpu.SemaphoreType.DMA((GROUP * heads,)),
            pltpu.SemaphoreType.DMA((GROUP * heads,)),
        ],
        input_output_aliases={GROUP: 0},
        compiler_params=PARAMS,
        name="later_rows",
    )(*pieces, rows)


def local(video_q, video_k, video_v, text_q, text_k, text_v, window_tiles, text_len):
    video, words = (video_q, video_k, video_v), (text_q, text_k, text_v)
    (f0, n0), (f1, n1) = CHUNKS
    (kv0,) = pack(video, [((1, 2), f0, n0, ROWS, True)])
    (text,) = pack(words, [((0, 1, 2), 0, HD, HALF, False)])
    kv1, q = pack(video, [((1, 2), f1, n1, ROWS, True), ((0,), 0, HD, ROWS, False)])
    own, before, after = [], [], []
    for kv in (kv0, kv1):
        own.append(swap(kv, "uly"))
        before.append(beside(own[-1], 1))
        after.append(beside(own[-1], -1))
    mine = exchange(text[:GROUP])
    other = [text[GROUP]]
    for d in range(1, GROUP):
        other.append(lax.ppermute(mine[d], "blk", [(i, i ^ 1) for i in range(BLK)]))
    text = mine + other
    q = exchange(q)
    slots = text_attention(text_len, text, own)
    slots = swap(slots, ("blk", "uly"))
    slots = combine(slots)
    slots = swap(slots, ("blk", "uly"))
    back = []
    for c, (first, heads) in enumerate(CHUNKS):
        o = video_attention(first, heads, window_tiles, text_len, q, text, before[c], own[c], after[c])
        back.append(exchange(o))
    rows, text_out = first_rows(back[0], slots, f0, n0)
    return later_rows(back[1], rows, f1, n1), text_out


def solution(mesh):
    in_specs = (
        P(("blk", "uly"), None),
        P(("blk", "uly"), None),
        P(("blk", "uly"), None),
        P("uly", None),
        P("uly", None),
        P("uly", None),
        P("blk", None),
        P(),
    )
    out_specs = (P(("blk", "uly"), None), P("uly", None))

    return jax.shard_map(local, mesh=mesh, in_specs=in_specs, out_specs=out_specs, check_vma=False)
```

```python
import functools
import math

import jax
import jax.numpy as jnp
from jax import lax
from jax.experimental import pallas as pl
from jax.experimental.pallas import tpu as pltpu
from jax.sharding import PartitionSpec as P


HEADS = 24
D = 128
TXT = 256
GROUP = 4
HD = HEADS // GROUP
ROWS = 288
SLICE = ROWS * GROUP
TILE = 384
TROWS = TXT // GROUP
HALF = TROWS // 2
BLK = 32
DEVS = GROUP * BLK
RB = 128
KEYS = 2 * SLICE + TXT
SCALE = math.log2(math.e) / math.sqrt(D)
CHUNKS = ((0, 4), (4, 2))
LIMIT = 67043328
BF = jnp.bfloat16
F32 = jnp.float32


ANY = pl.BlockSpec(memory_space=pl.ANY)
PARAMS = pltpu.CompilerParams(vmem_limit_bytes=LIMIT)
SMEM = pl.BlockSpec(memory_space=pltpu.SMEM)
VMEM = pl.BlockSpec(memory_space=pltpu.VMEM)


def place(distance):
    return (lax.axis_index("uly") + distance + GROUP) % GROUP


def half(which):
    return (lax.axis_index("blk") + which) % 2


def column(head):
    return pl.ds(pl.multiple_of(head * D, D), D)


def rows_of(position, count):
    return pl.ds(pl.multiple_of(position * count, 32), count)


def run(moves):
    for move in moves:
        move.start()


def wait(moves):
    for move in moves:
        move.wait()


def copy_list(pairs, sems):
    return [pltpu.make_async_copy(a, b, sems.at[i]) for i, (a, b) in enumerate(pairs)]


def pack(arrays, jobs):
    outs = []
    for numbers, _, heads, rows, together in jobs:
        shape = (len(numbers), heads, rows, D)
        if together:
            outs.append(jax.ShapeDtypeStruct((GROUP, *shape), BF))
        else:
            outs += [jax.ShapeDtypeStruct(shape, BF)] * (GROUP + (rows == HALF))

    def body(*refs):
        ins, rest = refs[: len(arrays)], refs[len(arrays) :]
        dst, held, in_sems, out_sems = rest[: len(outs)], rest[len(outs) : -2], rest[-2], rest[-1]
        reads, writes, n = [], [], 0
        for numbers, first, heads, rows, together in jobs:
            for d in range(GROUP + (rows == HALF)):
                which = slice(None) if rows == ROWS else rows_of(half(d // GROUP), rows)
                group = d if together else place(d % GROUP)
                here = held[n].at[d] if together else held[n]
                there = dst[n].at[d] if together else dst[n]
                pairs = [
                    (ins[k].at[which, column(group * HD + first + h)], here.at[i, h])
                    for i, k in enumerate(numbers)
                    for h in range(heads)
                ]
                base = sum(len(r) for r in reads)
                reads.append([pltpu.make_async_copy(x, y, in_sems.at[base + i]) for i, (x, y) in enumerate(pairs)])
                writes.append(pltpu.make_async_copy(here, there, out_sems.at[len(writes)]))
                n += not together
            n += together
        for read in reads:
            run(read)
        for read, write in zip(reads, writes):
            wait(read)
            write.start()
        wait(writes)

    got = pl.pallas_call(
        body,
        in_specs=[ANY] * len(arrays),
        out_specs=[ANY] * len(outs),
        out_shape=outs,
        scratch_shapes=[pltpu.VMEM(o.shape, BF) for o in outs]
        + [pltpu.SemaphoreType.DMA((160,)), pltpu.SemaphoreType.DMA((32,))],
        compiler_params=PARAMS,
    )(*arrays)
    result, n = [], 0
    for job in jobs:
        count = 1 if job[4] else GROUP + (job[3] == HALF)
        result.append(got[n] if job[4] else got[n : n + count])
        n += count
    return result


def around(block, distance):
    return lax.ppermute(block, "uly", [(i, (i + distance) % GROUP) for i in range(GROUP)])


def exchange(pieces):
    got = [pieces[0]]
    for d in range(1, GROUP):
        got.append(around(pieces[d], d))
    return got


def swap(array, axes):
    return lax.all_to_all(array, axes, 0, 0, tiled=True)


def beside(block, distance):
    return lax.ppermute(block, "blk", [(i, i + distance) for i in range(BLK) if 0 <= i + distance < BLK])


def text_bias(length):
    lane = lax.broadcasted_iota(jnp.int32, (1, TXT), 1)
    which = (lane // (TXT // 2) + half(0)) % 2
    source = (lax.axis_index("uly") + GROUP - lane % (TXT // 2) // HALF) % GROUP
    position = source * TROWS + which * HALF + lane % HALF
    return jnp.where(position < length, 0.0, -jnp.inf).astype(F32)


def weigh(q, keys, values, masked):
    s = lax.dot_general(q, keys(), (((1,), (1,)), ((), ())), preferred_element_type=F32)

    def finish():
        parts, at = [], 0
        for start, bias in masked:
            if start > at:
                parts.append(s[:, at:start])
            parts.append(s[:, start : start + TXT] + bias)
            at = start + TXT
        if at < s.shape[1]:
            parts.append(s[:, at:])
        whole = jnp.concatenate(parts, axis=1)
        top = jnp.max(whole, axis=1, keepdims=True) * SCALE
        p = jnp.exp2(whole * SCALE - top)
        total = jnp.sum(p, axis=1, keepdims=True)
        o = jnp.dot(p.astype(BF), values(), preferred_element_type=F32)
        return o / total, top + jnp.log2(total)

    return finish


SLOT = 16
PAIRS = 12


def text_body(length, *refs):
    text, kv, refs = refs[: 2 * GROUP], refs[2 * GROUP :][: len(CHUNKS)], refs[2 * GROUP + len(CHUNKS) :]
    out_ref, q_sc, kv_sc, o_sc, log_sc, sc, slots, sems = refs
    pairs, moves = [], []
    for n, piece in enumerate(text):
        rows = rows_of(2 * place(-(n % GROUP)) + half(n // GROUP), HALF)
        pairs.append((piece.at[0], q_sc.at[:, rows]))
        pairs.append((piece.at[pl.ds(1, 2)], kv_sc.at[:, :, pl.ds(SLICE + n * HALF, HALF)]))
    for c, (first, heads) in enumerate(CHUNKS):
        for g in range(GROUP):
            pairs.append((kv[c].at[g], kv_sc.at[:, pl.ds(first, heads), pl.ds(g * ROWS, ROWS)]))
        moves.append(copy_list(pairs, sems.at[c]))
        run(moves[-1])
        pairs = []
    sc[...] = jnp.zeros_like(sc)
    bias = jnp.where(lax.axis_index("blk") == 0, text_bias(length[0]), -jnp.inf)
    wait(moves[0])
    steps = [(h, i) for h in range(HD) for i in range(TXT // RB)]

    def begin(h, i):
        if (h, i) == (CHUNKS[1][0], 0):
            wait(moves[1])
        q = q_sc[h, i * RB : (i + 1) * RB]
        return weigh(q, lambda: kv_sc[0, h], lambda: kv_sc[1, h], [(SLICE, bias)])

    rest = begin(*steps[0])
    for n, (h, i) in enumerate(steps):
        following = begin(*steps[n + 1]) if n + 1 < len(steps) else None
        o, log = rest()
        o_sc[h, i * RB : (i + 1) * RB] = o
        log_sc[h, i * RB : (i + 1) * RB] = jnp.broadcast_to(log, (RB, D))
        rest = following
    lane = lax.broadcasted_iota(jnp.int32, (TROWS, D), 1)
    for p in range(2):
        logs = jnp.zeros((TROWS, D), F32)
        for u2 in range(GROUP):
            rows = pl.ds(u2 * TROWS, TROWS)
            for i in range(3):
                s = 3 * u2 + i
                sc[pl.ds(SLOT * p + s, TROWS, stride=2 * SLOT), :] = o_sc[3 * p + i, rows, :]
                logs = jnp.where(lane == s, log_sc[3 * p + i, rows, :], logs)
        for part in range(3):
            rounded = logs.astype(BF).astype(F32)
            sc[pl.ds(SLOT * p + PAIRS + part, TROWS, stride=2 * SLOT), :] = rounded
            logs = logs - rounded
    slots[...] = sc[...].astype(BF).reshape(DEVS, SLOT, D)
    leave(slots, out_ref, sems.at[0])


def leave(held, out_ref, sems):
    size = held.shape[0] // 4
    parts = [pl.ds(i * size, size) for i in range(4)]
    moves = copy_list([(held.at[x], out_ref.at[x]) for x in parts], sems)
    run(moves)
    wait(moves)


def text_attention(length, text, kv):
    return pl.pallas_call(
        text_body,
        in_specs=[SMEM] + [ANY] * (2 * GROUP + len(CHUNKS)),
        out_specs=ANY,
        out_shape=jax.ShapeDtypeStruct((DEVS, SLOT, D), BF),
        scratch_shapes=[
            pltpu.VMEM((HD, TXT, D), BF),
            pltpu.VMEM((2, HD, SLICE + TXT, D), BF),
            pltpu.VMEM((HD, TXT, D), F32),
            pltpu.VMEM((HD, TXT, D), F32),
            pltpu.VMEM((DEVS * SLOT, D), F32),
            pltpu.VMEM((DEVS, SLOT, D), BF),
            pltpu.SemaphoreType.DMA((2, 24)),
        ],
        compiler_params=PARAMS,
        name="text_attention",
    )(length, *text, *kv)


def combine_body(in_ref, out_ref, sc, res, slots, got, sems):
    leave(in_ref, got, sems)
    sc[...] = got[...].astype(F32).reshape(DEVS * SLOT, D)
    logs = sc[pl.ds(PAIRS, DEVS, stride=SLOT), :]
    for part in range(1, 3):
        logs = logs + sc[pl.ds(PAIRS + part, DEVS, stride=SLOT), :]
    logs = jnp.transpose(logs)[:SLOT]
    group = lax.broadcasted_iota(jnp.int32, (SLOT, DEVS), 1) % GROUP
    top = jnp.zeros((SLOT, DEVS), F32)
    for u in range(GROUP):
        best = jnp.max(jnp.where(group == u, logs, -jnp.inf), axis=1, keepdims=True)
        top = jnp.where(group == u, best, top)
    weights = jnp.exp2(logs - top)
    total = jnp.ones((SLOT, DEVS), F32)
    for u in range(GROUP):
        all_u = jnp.sum(jnp.where(group == u, weights, 0.0), axis=1, keepdims=True)
        total = jnp.where(group == u, all_u, total)
    weights = weights / total
    mine = lax.broadcasted_iota(jnp.int32, (8, DEVS), 1) % GROUP == lax.broadcasted_iota(jnp.int32, (8, DEVS), 0)
    res[...] = jnp.zeros_like(res)
    for u2 in range(GROUP):
        for i in range(3):
            s = 3 * u2 + i
            left = jnp.where(mine, jnp.broadcast_to(weights[s : s + 1], (8, DEVS)), 0.0)
            values = sc[pl.ds(s, DEVS, stride=SLOT), :]
            got = jnp.dot(left, values, preferred_element_type=F32, precision=lax.Precision.HIGHEST)
            for u in range(GROUP):
                res[u2, pl.ds(3 * u + i, 1), :] = got[u : u + 1]
    done = res[...].astype(BF)
    for b in range(BLK):
        slots[b] = done
    leave(slots, out_ref, sems)


def combine(received):
    return pl.pallas_call(
        combine_body,
        in_specs=[ANY],
        out_specs=ANY,
        out_shape=jax.ShapeDtypeStruct((BLK, GROUP, SLOT, D), BF),
        scratch_shapes=[
            pltpu.VMEM((DEVS * SLOT, D), F32),
            pltpu.VMEM((GROUP, SLOT, D), F32),
            pltpu.VMEM((BLK, GROUP, SLOT, D), BF),
            pltpu.VMEM((DEVS, SLOT, D), BF),
            pltpu.SemaphoreType.DMA((4,)),
        ],
        compiler_params=PARAMS,
        name="combine",
    )(received).reshape(DEVS, SLOT, D)


def video_body(first, heads, tiles, length, *refs):
    q_refs, text, refs = refs[:GROUP], refs[GROUP : 3 * GROUP], refs[3 * GROUP :]
    before, own, after, refs = refs[0], refs[1], refs[2], refs[3:]
    o_refs, refs = refs[:GROUP], refs[GROUP:]
    q_sc, k_sc, v_sc, o_sc, side_sc, sems, shared_sems, o_sems = refs

    def loads(start, count, a):
        some, pairs = pl.ds(start, count), []
        for base, kv in ((0, before), (SLICE, own), (KEYS, after)):
            for g in range(GROUP):
                pairs.append((kv.at[g, a, some], (k_sc, v_sc)[a].at[some, pl.ds(base + g * ROWS, ROWS)]))
        return copy_list(pairs, sems.at[min(start, 1), a])

    others = loads(1, heads - 1, 0) + loads(1, heads - 1, 1)
    asked = pl.ds(first, heads)
    shared = [[(q_refs[d].at[0, asked], q_sc.at[:, rows_of(place(-d), ROWS)]) for d in range(GROUP)], []]
    for a, sc in ((0, k_sc), (1, v_sc)):
        for n, piece in enumerate(text):
            shared[a].append((piece.at[1 + a, asked], sc.at[:, pl.ds(2 * SLICE + n * HALF, HALF)]))
    shared = [copy_list(pairs, shared_sems.at[a]) for a, pairs in enumerate(shared)]
    run(loads(0, 1, 0))
    run(shared[0])
    run(loads(0, 1, 1))
    run(shared[1])
    run(others)

    def stores(h):
        return [
            pltpu.make_async_copy(o_sc.at[h, rows_of(place(d), ROWS)], o_refs[d].at[h], o_sems.at[h, d])
            for d in range(GROUP)
        ]

    limit = (lax.axis_index("blk") + 1) * tiles.shape[0]
    for j in range(tiles.shape[0]):
        last = tiles[j, 0]
        for w in range(1, tiles.shape[1]):
            last = jnp.maximum(last, tiles[j, w])
        side_sc[j] = (last >= limit).astype(jnp.int32)
    live = text_bias(length[0])

    def step(h, i):
        f = side_sc[i * RB // TILE]
        window = pl.ds(pl.multiple_of(f * SLICE, RB), KEYS)
        masked = [(SLICE, jnp.where(f == 1, live, 0.0)), (2 * SLICE, jnp.where(f == 1, 0.0, live))]
        q = q_sc[h, i * RB : (i + 1) * RB, :]
        return weigh(q, lambda: k_sc[h, window], lambda: v_sc[h, window], masked)

    steps = SLICE // RB
    wait(loads(0, 1, 0) + shared[0])

    def one(h, _):
        @pl.when(h == 1)
        def _():
            wait(others)

        rest = step(h, 0)

        @pl.when(h == 0)
        def _():
            wait(loads(0, 1, 1) + shared[1])

        for i in range(steps):
            following = step(h, i + 1) if i + 1 < steps else None
            o, _ = rest()
            o_sc[h, i * RB : (i + 1) * RB, :] = o.astype(BF)
            rest = following
        run(stores(h))
        return 0

    lax.fori_loop(0, heads, one, 0)
    for h in range(heads):
        wait(stores(h))


def video_attention(first, heads, tiles, length, q, text, before, own, after):
    return pl.pallas_call(
        functools.partial(video_body, first, heads),
        in_specs=[SMEM, SMEM] + [ANY] * (3 * GROUP + 3),
        out_specs=[ANY] * GROUP,
        out_shape=[jax.ShapeDtypeStruct((heads, ROWS, D), BF)] * GROUP,
        scratch_shapes=[
            pltpu.VMEM((heads, SLICE, D), BF),
            pltpu.VMEM((heads, KEYS + SLICE, D), BF),
            pltpu.VMEM((heads, KEYS + SLICE, D), BF),
            pltpu.VMEM((heads, SLICE, D), BF),
            pltpu.SMEM((8,), jnp.int32),
            pltpu.SemaphoreType.DMA((2, 2, 12)),
            pltpu.SemaphoreType.DMA((2, 12)),
            pltpu.SemaphoreType.DMA((heads, GROUP)),
        ],
        compiler_params=PARAMS,
        name="video_attention",
    )(tiles, length, *q, *text, before, own, after)


def rows_body(first, heads, *refs):
    pieces, refs = refs[:GROUP], refs[-4:]
    video_out, held, in_sems, out_sems = refs
    reads, writes = [], []
    for d in range(GROUP):
        for h in range(heads):
            n = len(reads)
            reads.append(pltpu.make_async_copy(pieces[d].at[h], held.at[n], in_sems.at[n]))
            there = video_out.at[:, column(place(-d) * HD + first + h)]
            writes.append(pltpu.make_async_copy(held.at[n], there, out_sems.at[n]))
    run(reads)
    for read, write in zip(reads, writes):
        read.wait()
        write.start()
    return writes


def first_body(first, heads, *refs):
    pieces, slots, video_out, text_out, held, sc, got, in_sems, out_sems, sems = refs[:GROUP], *refs[GROUP:]
    fetch = pltpu.make_async_copy(slots, got, sems.at[0])
    fetch.start()
    writes = rows_body(first, heads, *pieces, video_out, held, in_sems, out_sems)
    fetch.wait()
    sc[...] = got[...].astype(F32).reshape(DEVS * SLOT, D)
    for p in range(2):
        for u in range(GROUP):
            for i in range(3):
                rows = sc[pl.ds(SLOT * p + 3 * u + i, TROWS, stride=2 * SLOT), :]
                head = HD * u + 3 * p + i
                text_out[:, head * D : (head + 1) * D] = rows.astype(BF)
    wait(writes)


def later_body(first, heads, *refs):
    wait(rows_body(first, heads, *refs))


def first_rows(pieces, slots, first, heads):
    return pl.pallas_call(
        functools.partial(first_body, first, heads),
        in_specs=[ANY] * (GROUP + 1),
        out_specs=[ANY, VMEM],
        out_shape=[
            jax.ShapeDtypeStruct((ROWS, HEADS * D), BF),
            jax.ShapeDtypeStruct((TROWS, HEADS * D), BF),
        ],
        scratch_shapes=[
            pltpu.VMEM((GROUP * heads, ROWS, D), BF),
            pltpu.VMEM((DEVS * SLOT, D), F32),
            pltpu.VMEM((DEVS, SLOT, D), BF),
            pltpu.SemaphoreType.DMA((GROUP * heads,)),
            pltpu.SemaphoreType.DMA((GROUP * heads,)),
            pltpu.SemaphoreType.DMA((4,)),
        ],
        compiler_params=PARAMS,
        name="first_rows",
    )(*pieces, slots)


def later_rows(pieces, rows, first, heads):
    return pl.pallas_call(
        functools.partial(later_body, first, heads),
        in_specs=[ANY] * (GROUP + 1),
        out_specs=ANY,
        out_shape=jax.ShapeDtypeStruct((ROWS, HEADS * D), BF),
        scratch_shapes=[
            pltpu.VMEM((GROUP * heads, ROWS, D), BF),
            pltpu.SemaphoreType.DMA((GROUP * heads,)),
            pltpu.SemaphoreType.DMA((GROUP * heads,)),
        ],
        input_output_aliases={GROUP: 0},
        compiler_params=PARAMS,
        name="later_rows",
    )(*pieces, rows)


def local(video_q, video_k, video_v, text_q, text_k, text_v, window_tiles, text_len):
    video, words = (video_q, video_k, video_v), (text_q, text_k, text_v)
    (f0, n0), (f1, n1) = CHUNKS
    (kv0,) = pack(video, [((1, 2), f0, n0, ROWS, True)])
    text, kv1, q = pack(
        video + words,
        [
            ((3, 4, 5), 0, HD, HALF, False),
            ((1, 2), f1, n1, ROWS, True),
            ((0,), 0, HD, ROWS, False),
        ],
    )
    own, before, after = [], [], []
    for kv in (kv0, kv1):
        own.append(swap(kv, "uly"))
        before.append(beside(own[-1], 1))
        after.append(beside(own[-1], -1))
    mine = exchange(text[:GROUP])
    other = [text[GROUP]]
    for d in range(1, GROUP):
        other.append(lax.ppermute(mine[d], "blk", [(i, i ^ 1) for i in range(BLK)]))
    text = mine + other
    q = exchange(q)
    slots = text_attention(text_len, text, own)
    slots = swap(slots, ("blk", "uly"))
    slots = combine(slots)
    slots = swap(slots, ("blk", "uly"))
    back = []
    for c, (first, heads) in enumerate(CHUNKS):
        o = video_attention(first, heads, window_tiles, text_len, q, text, before[c], own[c], after[c])
        back.append(exchange(o))
    rows, text_out = first_rows(back[0], slots, f0, n0)
    return later_rows(back[1], rows, f1, n1), text_out


def solution(mesh):
    in_specs = (
        P(("blk", "uly"), None),
        P(("blk", "uly"), None),
        P(("blk", "uly"), None),
        P("uly", None),
        P("uly", None),
        P("uly", None),
        P("blk", None),
        P(),
    )
    out_specs = (P(("blk", "uly"), None), P("uly", None))

    return jax.shard_map(local, mesh=mesh, in_specs=in_specs, out_specs=out_specs, check_vma=False)
```

```python
import functools
import math

import jax
import jax.numpy as jnp
from jax import lax
from jax.experimental import pallas as pl
from jax.experimental.pallas import tpu as pltpu
from jax.sharding import PartitionSpec as P


HEADS = 24
D = 128
TXT = 256
GROUP = 4
HD = HEADS // GROUP
ROWS = 288
SLICE = ROWS * GROUP
TILE = 384
TROWS = TXT // GROUP
HALF = TROWS // 2
BLK = 32
DEVS = GROUP * BLK
RB = 128
KEYS = 2 * SLICE + TXT
SCALE = math.log2(math.e) / math.sqrt(D)
CHUNKS = ((0, 4), (4, 2))
LIMIT = 67043328
BF = jnp.bfloat16
F32 = jnp.float32


ANY = pl.BlockSpec(memory_space=pl.ANY)
PARAMS = pltpu.CompilerParams(vmem_limit_bytes=LIMIT)
SMEM = pl.BlockSpec(memory_space=pltpu.SMEM)
VMEM = pl.BlockSpec(memory_space=pltpu.VMEM)


def place(distance):
    return (lax.axis_index("uly") + distance + GROUP) % GROUP


def half(which):
    return (lax.axis_index("blk") + which) % 2


def column(head):
    return pl.ds(pl.multiple_of(head * D, D), D)


def rows_of(position, count):
    return pl.ds(pl.multiple_of(position * count, 32), count)


def run(moves):
    for move in moves:
        move.start()


def wait(moves):
    for move in moves:
        move.wait()


def copy_list(pairs, sems):
    return [pltpu.make_async_copy(a, b, sems.at[i]) for i, (a, b) in enumerate(pairs)]


def pack(arrays, jobs):
    outs = []
    for numbers, _, heads, rows, together in jobs:
        shape = (len(numbers), heads, rows, D)
        if together:
            outs.append(jax.ShapeDtypeStruct((GROUP, *shape), BF))
        else:
            outs += [jax.ShapeDtypeStruct(shape, BF)] * (GROUP + (rows == HALF))

    def body(*refs):
        ins, rest = refs[: len(arrays)], refs[len(arrays) :]
        dst, held, in_sems, out_sems = rest[: len(outs)], rest[len(outs) : -2], rest[-2], rest[-1]
        reads, writes, n = [], [], 0
        for numbers, first, heads, rows, together in jobs:
            for d in range(GROUP + (rows == HALF)):
                which = slice(None) if rows == ROWS else rows_of(half(d // GROUP), rows)
                group = d if together else place(d % GROUP)
                here = held[n].at[d] if together else held[n]
                there = dst[n].at[d] if together else dst[n]
                for i, k in enumerate(numbers):
                    base = sum(len(r) for r in reads)
                    reads.append(
                        [
                            pltpu.make_async_copy(
                                ins[k].at[which, column(group * HD + first + h)],
                                here.at[i, h],
                                in_sems.at[base + h],
                            )
                            for h in range(heads)
                        ]
                    )
                    writes.append(pltpu.make_async_copy(here.at[i], there.at[i], out_sems.at[len(writes)]))
                n += not together
            n += together
        for read in reads:
            run(read)
        for read, write in zip(reads, writes):
            wait(read)
            write.start()
        wait(writes)

    got = pl.pallas_call(
        body,
        in_specs=[ANY] * len(arrays),
        out_specs=[ANY] * len(outs),
        out_shape=outs,
        scratch_shapes=[pltpu.VMEM(o.shape, BF) for o in outs]
        + [pltpu.SemaphoreType.DMA((160,)), pltpu.SemaphoreType.DMA((32,))],
        compiler_params=PARAMS,
    )(*arrays)
    result, n = [], 0
    for job in jobs:
        count = 1 if job[4] else GROUP + (job[3] == HALF)
        result.append(got[n] if job[4] else got[n : n + count])
        n += count
    return result


def around(block, distance):
    return lax.ppermute(block, "uly", [(i, (i + distance) % GROUP) for i in range(GROUP)])


def exchange(pieces):
    got = [pieces[0]]
    for d in range(1, GROUP):
        got.append(around(pieces[d], d))
    return got


def swap(array, axes):
    return lax.all_to_all(array, axes, 0, 0, tiled=True)


def beside(block, distance):
    return lax.ppermute(block, "blk", [(i, i + distance) for i in range(BLK) if 0 <= i + distance < BLK])


def text_bias(length):
    lane = lax.broadcasted_iota(jnp.int32, (1, TXT), 1)
    which = (lane // (TXT // 2) + half(0)) % 2
    source = (lax.axis_index("uly") + GROUP - lane % (TXT // 2) // HALF) % GROUP
    position = source * TROWS + which * HALF + lane % HALF
    return jnp.where(position < length, 0.0, -jnp.inf).astype(F32)


def weigh(q, keys, values, masked):
    s = lax.dot_general(q, keys(), (((1,), (1,)), ((), ())), preferred_element_type=F32)

    def finish():
        parts, at = [], 0
        for start, bias in masked:
            if start > at:
                parts.append(s[:, at:start])
            parts.append(s[:, start : start + TXT] + bias)
            at = start + TXT
        if at < s.shape[1]:
            parts.append(s[:, at:])
        whole = jnp.concatenate(parts, axis=1)
        top = jnp.max(whole, axis=1, keepdims=True) * SCALE
        p = jnp.exp2(whole * SCALE - top)
        total = jnp.sum(p, axis=1, keepdims=True)
        o = jnp.dot(p.astype(BF), values(), preferred_element_type=F32)
        return o / total, top + jnp.log2(total)

    return finish


SLOT = 16
PAIRS = 12


def text_body(length, *refs):
    text, kv, refs = refs[: 2 * GROUP], refs[2 * GROUP :][: len(CHUNKS)], refs[2 * GROUP + len(CHUNKS) :]
    out_ref, q_sc, kv_sc, o_sc, log_sc, sc, slots, sems = refs
    pairs, moves = [], []
    for n, piece in enumerate(text):
        rows = rows_of(2 * place(-(n % GROUP)) + half(n // GROUP), HALF)
        pairs.append((piece.at[0], q_sc.at[:, rows]))
        pairs.append((piece.at[pl.ds(1, 2)], kv_sc.at[:, :, pl.ds(SLICE + n * HALF, HALF)]))
    for c, (first, heads) in enumerate(CHUNKS):
        for g in range(GROUP):
            pairs.append((kv[c].at[g], kv_sc.at[:, pl.ds(first, heads), pl.ds(g * ROWS, ROWS)]))
        moves.append(copy_list(pairs, sems.at[c]))
        run(moves[-1])
        pairs = []
    sc[...] = jnp.zeros_like(sc)
    bias = jnp.where(lax.axis_index("blk") == 0, text_bias(length[0]), -jnp.inf)
    wait(moves[0])
    steps = [(h, i) for h in range(HD) for i in range(TXT // RB)]

    def begin(h, i):
        if (h, i) == (CHUNKS[1][0], 0):
            wait(moves[1])
        q = q_sc[h, i * RB : (i + 1) * RB]
        return weigh(q, lambda: kv_sc[0, h], lambda: kv_sc[1, h], [(SLICE, bias)])

    rest = begin(*steps[0])
    for n, (h, i) in enumerate(steps):
        following = begin(*steps[n + 1]) if n + 1 < len(steps) else None
        o, log = rest()
        o_sc[h, i * RB : (i + 1) * RB] = o
        log_sc[h, i * RB : (i + 1) * RB] = jnp.broadcast_to(log, (RB, D))
        rest = following
    lane = lax.broadcasted_iota(jnp.int32, (TROWS, D), 1)
    for p in range(2):
        logs = jnp.zeros((TROWS, D), F32)
        for u2 in range(GROUP):
            rows = pl.ds(u2 * TROWS, TROWS)
            for i in range(3):
                s = 3 * u2 + i
                sc[pl.ds(SLOT * p + s, TROWS, stride=2 * SLOT), :] = o_sc[3 * p + i, rows, :]
                logs = jnp.where(lane == s, log_sc[3 * p + i, rows, :], logs)
        for part in range(3):
            rounded = logs.astype(BF).astype(F32)
            sc[pl.ds(SLOT * p + PAIRS + part, TROWS, stride=2 * SLOT), :] = rounded
            logs = logs - rounded
    slots[...] = sc[...].astype(BF).reshape(DEVS, SLOT, D)
    leave(slots, out_ref, sems.at[0])


def leave(held, out_ref, sems):
    size = held.shape[0] // 4
    parts = [pl.ds(i * size, size) for i in range(4)]
    moves = copy_list([(held.at[x], out_ref.at[x]) for x in parts], sems)
    run(moves)
    wait(moves)


def text_attention(length, text, kv):
    return pl.pallas_call(
        text_body,
        in_specs=[SMEM] + [ANY] * (2 * GROUP + len(CHUNKS)),
        out_specs=ANY,
        out_shape=jax.ShapeDtypeStruct((DEVS, SLOT, D), BF),
        scratch_shapes=[
            pltpu.VMEM((HD, TXT, D), BF),
            pltpu.VMEM((2, HD, SLICE + TXT, D), BF),
            pltpu.VMEM((HD, TXT, D), F32),
            pltpu.VMEM((HD, TXT, D), F32),
            pltpu.VMEM((DEVS * SLOT, D), F32),
            pltpu.VMEM((DEVS, SLOT, D), BF),
            pltpu.SemaphoreType.DMA((2, 24)),
        ],
        compiler_params=PARAMS,
        name="text_attention",
    )(length, *text, *kv)


def combine_body(in_ref, out_ref, sc, res, slots, got, sems):
    leave(in_ref, got, sems)
    sc[...] = got[...].astype(F32).reshape(DEVS * SLOT, D)
    logs = sc[pl.ds(PAIRS, DEVS, stride=SLOT), :]
    for part in range(1, 3):
        logs = logs + sc[pl.ds(PAIRS + part, DEVS, stride=SLOT), :]
    logs = jnp.transpose(logs)[:SLOT]
    group = lax.broadcasted_iota(jnp.int32, (SLOT, DEVS), 1) % GROUP
    top = jnp.zeros((SLOT, DEVS), F32)
    for u in range(GROUP):
        best = jnp.max(jnp.where(group == u, logs, -jnp.inf), axis=1, keepdims=True)
        top = jnp.where(group == u, best, top)
    weights = jnp.exp2(logs - top)
    total = jnp.ones((SLOT, DEVS), F32)
    for u in range(GROUP):
        all_u = jnp.sum(jnp.where(group == u, weights, 0.0), axis=1, keepdims=True)
        total = jnp.where(group == u, all_u, total)
    weights = weights / total
    mine = lax.broadcasted_iota(jnp.int32, (8, DEVS), 1) % GROUP == lax.broadcasted_iota(jnp.int32, (8, DEVS), 0)
    res[...] = jnp.zeros_like(res)
    for u2 in range(GROUP):
        for i in range(3):
            s = 3 * u2 + i
            left = jnp.where(mine, jnp.broadcast_to(weights[s : s + 1], (8, DEVS)), 0.0)
            values = sc[pl.ds(s, DEVS, stride=SLOT), :]
            got = jnp.dot(left, values, preferred_element_type=F32, precision=lax.Precision.HIGHEST)
            for u in range(GROUP):
                res[u2, pl.ds(3 * u + i, 1), :] = got[u : u + 1]
    done = res[...].astype(BF)
    for b in range(BLK):
        slots[b] = done
    leave(slots, out_ref, sems)


def combine(received):
    return pl.pallas_call(
        combine_body,
        in_specs=[ANY],
        out_specs=ANY,
        out_shape=jax.ShapeDtypeStruct((BLK, GROUP, SLOT, D), BF),
        scratch_shapes=[
            pltpu.VMEM((DEVS * SLOT, D), F32),
            pltpu.VMEM((GROUP, SLOT, D), F32),
            pltpu.VMEM((BLK, GROUP, SLOT, D), BF),
            pltpu.VMEM((DEVS, SLOT, D), BF),
            pltpu.SemaphoreType.DMA((4,)),
        ],
        compiler_params=PARAMS,
        name="combine",
    )(received).reshape(DEVS, SLOT, D)


def video_body(first, heads, tiles, length, *refs):
    q_refs, text, refs = refs[:GROUP], refs[GROUP : 3 * GROUP], refs[3 * GROUP :]
    before, own, after, refs = refs[0], refs[1], refs[2], refs[3:]
    o_refs, refs = refs[:GROUP], refs[GROUP:]
    q_sc, k_sc, v_sc, o_sc, side_sc, sems, shared_sems, o_sems = refs

    def loads(start, count, a):
        some, pairs = pl.ds(start, count), []
        for base, kv in ((0, before), (SLICE, own), (KEYS, after)):
            for g in range(GROUP):
                pairs.append((kv.at[g, a, some], (k_sc, v_sc)[a].at[some, pl.ds(base + g * ROWS, ROWS)]))
        return copy_list(pairs, sems.at[min(start, 1), a])

    others = loads(1, heads - 1, 0) + loads(1, heads - 1, 1)
    asked = pl.ds(first, heads)
    shared = [[(q_refs[d].at[0, asked], q_sc.at[:, rows_of(place(-d), ROWS)]) for d in range(GROUP)], []]
    for a, sc in ((0, k_sc), (1, v_sc)):
        for n, piece in enumerate(text):
            shared[a].append((piece.at[1 + a, asked], sc.at[:, pl.ds(2 * SLICE + n * HALF, HALF)]))
    shared = [copy_list(pairs, shared_sems.at[a]) for a, pairs in enumerate(shared)]
    run(loads(0, 1, 0))
    run(shared[0])
    run(loads(0, 1, 1))
    run(shared[1])
    run(others)

    def stores(h):
        return [
            pltpu.make_async_copy(o_sc.at[h, rows_of(place(d), ROWS)], o_refs[d].at[h], o_sems.at[h, d])
            for d in range(GROUP)
        ]

    limit = (lax.axis_index("blk") + 1) * tiles.shape[0]
    for j in range(tiles.shape[0]):
        last = tiles[j, 0]
        for w in range(1, tiles.shape[1]):
            last = jnp.maximum(last, tiles[j, w])
        side_sc[j] = (last >= limit).astype(jnp.int32)
    live = text_bias(length[0])

    def step(h, i):
        f = side_sc[i * RB // TILE]
        window = pl.ds(pl.multiple_of(f * SLICE, RB), KEYS)
        masked = [(SLICE, jnp.where(f == 1, live, 0.0)), (2 * SLICE, jnp.where(f == 1, 0.0, live))]
        q = q_sc[h, i * RB : (i + 1) * RB, :]
        return weigh(q, lambda: k_sc[h, window], lambda: v_sc[h, window], masked)

    steps = SLICE // RB
    wait(loads(0, 1, 0) + shared[0])

    def one(h, _):
        @pl.when(h == 1)
        def _():
            wait(others)

        rest = step(h, 0)

        @pl.when(h == 0)
        def _():
            wait(loads(0, 1, 1) + shared[1])

        for i in range(steps):
            following = step(h, i + 1) if i + 1 < steps else None
            o, _ = rest()
            o_sc[h, i * RB : (i + 1) * RB, :] = o.astype(BF)
            rest = following
        run(stores(h))
        return 0

    lax.fori_loop(0, heads, one, 0)
    for h in range(heads):
        wait(stores(h))


def video_attention(first, heads, tiles, length, q, text, before, own, after):
    return pl.pallas_call(
        functools.partial(video_body, first, heads),
        in_specs=[SMEM, SMEM] + [ANY] * (3 * GROUP + 3),
        out_specs=[ANY] * GROUP,
        out_shape=[jax.ShapeDtypeStruct((heads, ROWS, D), BF)] * GROUP,
        scratch_shapes=[
            pltpu.VMEM((heads, SLICE, D), BF),
            pltpu.VMEM((heads, KEYS + SLICE, D), BF),
            pltpu.VMEM((heads, KEYS + SLICE, D), BF),
            pltpu.VMEM((heads, SLICE, D), BF),
            pltpu.SMEM((8,), jnp.int32),
            pltpu.SemaphoreType.DMA((2, 2, 12)),
            pltpu.SemaphoreType.DMA((2, 12)),
            pltpu.SemaphoreType.DMA((heads, GROUP)),
        ],
        compiler_params=PARAMS,
        name="video_attention",
    )(tiles, length, *q, *text, before, own, after)


def rows_body(first, heads, *refs):
    pieces, refs = refs[:GROUP], refs[-4:]
    video_out, held, in_sems, out_sems = refs
    reads, writes = [], []
    for d in range(GROUP):
        for h in range(heads):
            n = len(reads)
            reads.append(pltpu.make_async_copy(pieces[d].at[h], held.at[n], in_sems.at[n]))
            there = video_out.at[:, column(place(-d) * HD + first + h)]
            writes.append(pltpu.make_async_copy(held.at[n], there, out_sems.at[n]))
    run(reads)
    for read, write in zip(reads, writes):
        read.wait()
        write.start()
    return writes


def first_body(first, heads, *refs):
    pieces, slots, video_out, text_out, held, sc, got, in_sems, out_sems, sems = refs[:GROUP], *refs[GROUP:]
    fetch = pltpu.make_async_copy(slots, got, sems.at[0])
    fetch.start()
    writes = rows_body(first, heads, *pieces, video_out, held, in_sems, out_sems)
    fetch.wait()
    sc[...] = got[...].astype(F32).reshape(DEVS * SLOT, D)
    for p in range(2):
        for u in range(GROUP):
            for i in range(3):
                rows = sc[pl.ds(SLOT * p + 3 * u + i, TROWS, stride=2 * SLOT), :]
                head = HD * u + 3 * p + i
                text_out[:, head * D : (head + 1) * D] = rows.astype(BF)
    wait(writes)


def later_body(first, heads, *refs):
    wait(rows_body(first, heads, *refs))


def first_rows(pieces, slots, first, heads):
    return pl.pallas_call(
        functools.partial(first_body, first, heads),
        in_specs=[ANY] * (GROUP + 1),
        out_specs=[ANY, VMEM],
        out_shape=[
            jax.ShapeDtypeStruct((ROWS, HEADS * D), BF),
            jax.ShapeDtypeStruct((TROWS, HEADS * D), BF),
        ],
        scratch_shapes=[
            pltpu.VMEM((GROUP * heads, ROWS, D), BF),
            pltpu.VMEM((DEVS * SLOT, D), F32),
            pltpu.VMEM((DEVS, SLOT, D), BF),
            pltpu.SemaphoreType.DMA((GROUP * heads,)),
            pltpu.SemaphoreType.DMA((GROUP * heads,)),
            pltpu.SemaphoreType.DMA((4,)),
        ],
        compiler_params=PARAMS,
        name="first_rows",
    )(*pieces, slots)


def later_rows(pieces, rows, first, heads):
    return pl.pallas_call(
        functools.partial(later_body, first, heads),
        in_specs=[ANY] * (GROUP + 1),
        out_specs=ANY,
        out_shape=jax.ShapeDtypeStruct((ROWS, HEADS * D), BF),
        scratch_shapes=[
            pltpu.VMEM((GROUP * heads, ROWS, D), BF),
            pltpu.SemaphoreType.DMA((GROUP * heads,)),
            pltpu.SemaphoreType.DMA((GROUP * heads,)),
        ],
        input_output_aliases={GROUP: 0},
        compiler_params=PARAMS,
        name="later_rows",
    )(*pieces, rows)


def local(video_q, video_k, video_v, text_q, text_k, text_v, window_tiles, text_len):
    video, words = (video_q, video_k, video_v), (text_q, text_k, text_v)
    (f0, n0), (f1, n1) = CHUNKS
    (kv0,) = pack(video, [((1, 2), f0, n0, ROWS, True)])
    text, kv1, q = pack(
        video + words,
        [
            ((3, 4, 5), 0, HD, HALF, False),
            ((1, 2), f1, n1, ROWS, True),
            ((0,), 0, HD, ROWS, False),
        ],
    )
    own, before, after = [], [], []
    for kv in (kv0, kv1):
        own.append(swap(kv, "uly"))
        before.append(beside(own[-1], 1))
        after.append(beside(own[-1], -1))
    mine = exchange(text[:GROUP])
    other = [text[GROUP]]
    for d in range(1, GROUP):
        other.append(lax.ppermute(mine[d], "blk", [(i, i ^ 1) for i in range(BLK)]))
    text = mine + other
    q = exchange(q)
    slots = text_attention(text_len, text, own)
    slots = swap(slots, ("blk", "uly"))
    slots = combine(slots)
    slots = swap(slots, ("blk", "uly"))
    back = []
    for c, (first, heads) in enumerate(CHUNKS):
        o = video_attention(first, heads, window_tiles, text_len, q, text, before[c], own[c], after[c])
        back.append(exchange(o))
    rows, text_out = first_rows(back[0], slots, f0, n0)
    return later_rows(back[1], rows, f1, n1), text_out


def solution(mesh):
    in_specs = (
        P(("blk", "uly"), None),
        P(("blk", "uly"), None),
        P(("blk", "uly"), None),
        P("uly", None),
        P("uly", None),
        P("uly", None),
        P("blk", None),
        P(),
    )
    out_specs = (P(("blk", "uly"), None), P("uly", None))

    return jax.shard_map(local, mesh=mesh, in_specs=in_specs, out_specs=out_specs, check_vma=False)
```
